32 devices in a mesh: row: 4 (over z), col: 8 (over y, x, core).
Axes of the slice: x: 2, y: 2, z: 4, core: 2. Of those that a mesh axis runs over, the one named last changes fastest.
Arguments:
- embedding: float32 [4096, 256], P(('row', 'col')), may hold values from -6 to 6
- seed_cluster: int32 [4096], P(('row', 'col')), may hold values from 0 to 127
Outputs:
- log_member: float32 [4096, 128], P(('row', 'col'))
The draws below stay inside these ranges and needn't reach their ends.
All inputs are finite; a program needn't handle non-finite values.
Results may differ from the reference program's by a relative error of at most 0.0003.
Values sent between devices are 32-bit elements; how exact they have to be, the bound alone decides.
A program may use at most 64 MiB of HBM per device.

```python
import jax
import jax.numpy as jnp
from jax import lax

FEATURES = 256
CLUSTER_COUNT = 128
POINTS_DEV = 128
SWEEPS = 2
POINTS = 4096
N_COL = 8


def set_ends(result, own_key, smallest, top_value):
    longest = result.shape.index(max(result.shape))
    spots = []
    for shift in (0, 1):
        where = [jax.random.randint(jax.random.fold_in(own_key, axis), (), 0, length) for axis, length in enumerate(result.shape)]
        where[longest] = (where[longest] + shift) % result.shape[longest]
        spots.append(tuple(where))
    return result.at[spots[0]].set(smallest).at[spots[1]].set(top_value)


def block_scale(rng, dims, shards, least, top_value):
    level = 1.0
    for axis_at, parts in shards:
        steps = jax.random.uniform(jax.random.fold_in(jax.random.fold_in(rng, 6), axis_at), (parts,), jnp.float32, least / len(shards), top_value / len(shards))
        level = level * jnp.repeat(jnp.exp(steps), dims[axis_at] // parts).reshape((-1,) + (1,) * (len(dims) - 1 - axis_at))
    return level


def centred(stream_key, shape, spread, limit, shards=(), kind=jnp.bfloat16):
    entries = spread * jax.random.normal(stream_key, shape, jnp.float32)
    if shards:
        entries = entries * block_scale(stream_key, shape, shards, -0.22, 0.18)
    return jnp.clip(entries, -limit, limit).astype(kind)


def setup_inputs(seed: int = 0) -> dict:
    streams_of = jax.random.split(jax.random.key(seed), 3)
    return {
        "embedding": centred(streams_of[0], (POINTS, FEATURES), 1.0, 6.0, ((0, 32),), jnp.float32),
        "seed_cluster": set_ends(jax.random.randint(streams_of[1], (POINTS,), 0, CLUSTER_COUNT), jax.random.fold_in(streams_of[1], 1), 0, CLUSTER_COUNT - 1).astype(jnp.int32),
    }


ANNEAL_TEMP_VALUE = 0.02

def reference(embedding, seed_cluster):
    total = embedding.shape[0]
    squared_norms = lax.optimization_barrier(jnp.sum(embedding * embedding, axis=1))
    cluster_labels = jnp.arange(CLUSTER_COUNT, dtype=jnp.int32)
    member = 0.5 * (seed_cluster[:, None] == cluster_labels[None, :]).astype(jnp.float32) + 0.5 / CLUSTER_COUNT
    height = POINTS_DEV * N_COL
    blocks_x = embedding.reshape(total // height, height, FEATURES)
    blocks_s = squared_norms.reshape(total // height, height)
    log_member = jnp.zeros((total, CLUSTER_COUNT), jnp.float32)
    for sweep in range(SWEEPS):

        def single_block(pair):
            rows, row_sq = pair
            inner = jnp.dot(rows, embedding.T, precision=lax.Precision.HIGHEST)
            distance = jnp.sqrt(row_sq[:, None] + squared_norms[None, :] - 2.0 * inner + 1.0)
            return jnp.dot(distance, member, precision=lax.Precision.HIGHEST)
        attraction = lax.map(single_block, (blocks_x, blocks_s)).reshape(total, CLUSTER_COUNT)
        counts = lax.optimization_barrier(jnp.sum(member, axis=0))
        cohesion = lax.optimization_barrier(jnp.sum(member * attraction, axis=0))
        pair_energy = attraction / counts[None, :] - cohesion[None, :] / (2.0 * counts[None, :] ** 2)
        member_logits = -pair_energy / ANNEAL_TEMP_VALUE
        highest = lax.optimization_barrier(jnp.max(member_logits, axis=1, keepdims=True))
        log_member = member_logits - highest - jnp.log(lax.optimization_barrier(jnp.sum(jnp.exp(member_logits - highest), axis=1, keepdims=True)))
        member = jnp.exp(log_member)
    return log_member
```

```python
import functools

import jax
import jax.numpy as jnp
from jax import lax
from jax.experimental import pallas as pl
from jax.experimental.pallas import tpu as pltpu
from jax.sharding import PartitionSpec as P

CLUSTER_COUNT = 128
SWEEPS = 2
ANNEAL_TEMP_VALUE = 0.02
MESH = pl.DeviceIdType.MESH
F32, BF16, I32 = jnp.float32, jnp.bfloat16, jnp.int32


def plane_order(R):
    return [2, 0, 3, 1] if R == 4 else list(range(R))


def flip(index, offset, size):
    out, bit = 0, 1
    while bit < size:
        out = out + bit * ((index // bit + offset // bit) % 2)
        bit *= 2
    return out


def look_up(index, values):
    out = jnp.int32(values[0])
    for i, value in enumerate(values):
        if i:
            out = jnp.where(index == i, jnp.int32(value), out)
    return out


def split2(x):
    first = x.astype(BF16)
    return first, (x - first.astype(F32)).astype(BF16)


def nt(a, b):
    return lax.dot_general(a, b, (((1,), (1,)), ((), ())), preferred_element_type=F32)


def tn(a, b):
    return lax.dot_general(a, b, (((0,), (0,)), ((), ())), preferred_element_type=F32)


def nn(a, b):
    return jnp.dot(a, b, preferred_element_type=F32)


def seeds_to_member(seeds):
    points = seeds.shape[1]
    labels = lax.broadcasted_iota(I32, (CLUSTER_COUNT, points), 0)
    chosen = jnp.where(labels == seeds, 0.5, 0.0).astype(F32)
    return chosen.T + 0.5 / CLUSTER_COUNT


def kernel(
    R, C, e_hbm, s_hbm, o_ref,
    e_row, s_row, e_blk, s_blk, eh, el, rsq, xt, csq, dhl, mp, mf, m32, early,
    hrow, hz, hcoh, cs, cr, pp, pin, psum, rin, a_own, a_row, a_blk, az_own, az_in,
    in_sem, ed_s, ed_r, er_s, er_r, eb_s, eb_r, sd_s, sd_r, sr_s, sr_r, sb_s, sb_r,
    cz_s, cz_r, px_s, px_r, rs_s, rs_r, az_s, az_r, ad_s, ad_r, ar_s, ar_r, ab_s, ab_r,
):
    n = e_hbm.shape[0]
    k = CLUSTER_COUNT
    Q = C // 2
    full = (R - 1) // 2
    has_half = R % 2 == 0
    half = 1 + full
    r = lax.axis_index("row")
    c = lax.axis_index("col")
    q, b = c // 2, c % 2
    order = plane_order(R)
    place = [order.index(i) for i in range(R)]
    guest_of = {f: look_up(r, [order[(place[i] + f) % R] for i in range(R)]) for f in range(1, half + 1)}
    host_of = {f: look_up(r, [order[(place[i] - f) % R] for i in range(R)]) for f in range(1, half + 1)}
    is_host = look_up(r, [int(place[i] < R // 2) for i in range(R)]) == 1
    is_guest = look_up(r, [int(place[i] < R // 2) for i in range(R)]) == 0
    fulls = list(range(1, full + 1))
    started = []

    def remote(src, dst, ssem, rsem, row, col):
        return pltpu.make_async_remote_copy(
            src_ref=src, dst_ref=dst, send_sem=ssem, recv_sem=rsem,
            device_id=(row, col), device_id_type=MESH,
        )

    def send(*args):
        copy = remote(*args)
        copy.start()
        started.append(copy)
        return copy

    def row_peer(t):
        return flip(r, t, R)

    def chip_peer(s):
        return flip(q, s, Q) * 2 + b

    partner = q * 2 + (1 - b)

    def row_slot(s, core):
        at = (2 * s + core) * n
        return pl.ds(at if isinstance(at, int) else pl.multiple_of(at, n), n)

    def pair_slot(s):
        return pl.ds(2 * s * n, 2 * n)

    barrier = pltpu.get_barrier_semaphore()
    for s in range(1, Q):
        pl.semaphore_signal(barrier, inc=1, device_id=(r, chip_peer(s)), device_id_type=MESH)
    pl.semaphore_signal(barrier, inc=1, device_id=(r, partner), device_id_type=MESH)
    for t in range(1, R):
        pl.semaphore_signal(barrier, inc=1, device_id=(row_peer(t), c), device_id_type=MESH)

    mine = row_slot(0, b)
    own_e = pltpu.make_async_copy(e_hbm, e_row.at[mine], in_sem.at[0])
    own_s = pltpu.make_async_copy(s_hbm, s_row.at[b], in_sem.at[1])
    own_e.start()
    own_s.start()
    if has_half:
        hrow[...] = jnp.zeros_like(hrow)
        hz[...] = jnp.zeros_like(hz)
        hcoh[...] = jnp.zeros_like(hcoh)

    pl.semaphore_wait(barrier, Q + R - 1)

    def spread(src_of, row_dst, blk_dst, d_s, d_r, b_s, b_r):
        direct, guests, halves = {}, {}, []
        if has_half:
            out = [
                remote(src, dst(half - 1), ss.at[half - 1], rs.at[half - 1], host_of[half], c)
                for src, dst, ss, rs in zip(src_of, blk_dst, b_s, b_r)
            ]

            @pl.when(is_guest)
            def _():
                for copy in out:
                    copy.start()

            halves = out
        for s in [0] + list(range(1, Q)):
            direct[s] = [
                send(src, dst(s), ss.at[s], rs.at[s], r, chip_peer(s) if s else partner)
                for src, dst, ss, rs in zip(src_of, row_dst, d_s, d_r)
            ]
            if s + 1 in fulls:
                f = s + 1
                guests[f] = [
                    send(src, dst(f - 1), ss.at[f - 1], rs.at[f - 1], host_of[f], c)
                    for src, dst, ss, rs in zip(src_of, blk_dst, b_s, b_r)
                ]
        for f in fulls:
            if f not in guests:
                guests[f] = [
                    send(src, dst(f - 1), ss.at[f - 1], rs.at[f - 1], host_of[f], c)
                    for src, dst, ss, rs in zip(src_of, blk_dst, b_s, b_r)
                ]
        return direct, guests, halves

    def hear(copies):
        for copy in copies:
            copy.wait_recv()

    e_direct, e_guest, e_half = spread(
        (s_hbm, e_hbm),
        (lambda s: s_row.at[2 * s + b], lambda s: e_row.at[row_slot(s, b)]),
        (lambda f: s_blk.at[f], lambda f: e_blk.at[f]),
        (sd_s, ed_s), (sd_r, ed_r), (sb_s, eb_s), (sb_r, eb_r),
    )

    def e_relay(s):
        hear(e_direct[s])
        at = row_slot(s, b)
        return [
            send(s_row.at[2 * s + b], s_row.at[2 * s + b], sr_s.at[s], sr_r.at[s], r, partner),
            send(e_row.at[at], e_row.at[at], er_s.at[s], er_r.at[s], r, partner),
        ]

    def ready_block(t, x, member):
        p1, p2 = split2(-2.0 * x)
        xt[t, :n, :] = p1
        xt[t, n:, :] = p2
        q1, q2 = split2(x * x)
        ones = jnp.ones((8, x.shape[1]), BF16)
        csq[t] = nt(ones, q2) + nt(ones, q1) + 1.0
        m32[t] = member
        if t:
            m = member.astype(BF16)
            mf[t - 1, :n, :k] = m
            mf[t - 1, n:, :k] = m

    def ready_guest(t):
        ready_block(t, e_blk[t - 1], seeds_to_member(s_blk[t - 1]))

    def ready_rows(s):
        at = pair_slot(s)
        x = e_row[at, :]
        p1, p2 = split2(x)
        eh[at, :] = p1
        el[at, :] = p2
        rsq[at, :] = jnp.sum(x * x, axis=1, keepdims=True)
        for core in range(2):
            mp[row_slot(s, core), :k] = seeds_to_member(s_row[2 * s + core]).astype(BF16)

    def tile(t, s):
        at = pair_slot(s)
        both = nt(eh[at, :], xt[t])
        inner = both[:, :n] + (both[:, n:] + nt(el[at, :], xt[t, :n, :]))
        p1, p2 = split2(jnp.sqrt(rsq[at, :] + csq[t, 0:1, :] + inner))
        dhl[t, at, :n] = p1
        dhl[t, at, n:] = p2

    def rows_of(w, t, s):
        d = dhl[t, pair_slot(s), :]
        if w == 0:
            return nn(d, mf[t - 1, :, :k])
        both = nn(d, mf[t - 1])
        return both[:, :k] + both[:, k:]

    def block_of(w, t, first, last):
        at = pl.ds(2 * first * n, 2 * (last - first) * n)
        d = dhl[t, at, :]
        if w == 0:
            both = tn(d, mp[at, :k])
            return both[:n] + both[n:]
        both = tn(d, mp[at, :])
        return both[:n, :k] + (both[n:, :k] + both[:n, k:])

    last = Q - 1
    sums = {}

    class Sweep:
        def __init__(self, w):
            self.w, self.exchange, self.scatter, self.out, self.shares = w, {}, {}, {}, {}

        def rows(self, s):
            w = self.w
            part = hrow[s] if has_half else 0.0
            for f in fulls:
                part = part + rows_of(w, f, s)
            pp[w, s, 0] = part[:n]
            pp[w, s, 1] = part[n:]
            self.exchange[s] = send(pp.at[w, s, 1 - b], pin.at[w, s], px_s.at[w, s], px_r.at[w, s], r, partner)

        def combine(self, s):
            w = self.w
            self.exchange[s].wait_recv()
            psum[w, s] = pp[w, s, b] + pin[w, s]
            if s:
                self.scatter[s] = send(
                    psum.at[w, s], rin.at[w, s], rs_s.at[w, s], rs_r.at[w, s], r, chip_peer(s)
                )

        def block_copy(self, t):
            w = self.w
            return remote(cs.at[w, t - 1], cr.at[w, t - 1], cz_s.at[w, t - 1], cz_r.at[w, t - 1], guest_of[t], c)

        def block(self, t):
            w = self.w
            part = early[t] + block_of(w, t, last, Q)
            cs[w, t - 1] = part
            copy = self.block_copy(t)
            copy.start()
            return 2.0 * jnp.sum(m32[t] * part, axis=0, keepdims=True)

        def blocks(self):
            if has_half:
                @pl.when(is_host)
                def _():
                    hcoh[...] = self.block(half)
            cohesion = hcoh[...] if has_half else 0.0
            for f in fulls:
                cohesion = cohesion + self.block(f)
                self.out[f] = self.block_copy(f)
                started.append(self.out[f])
            return cohesion

        def share(self, cohesion):
            w = self.w
            own = early[0] + block_of(w, 0, last, Q)
            cohesion = cohesion + jnp.sum(m32[0] * own, axis=0, keepdims=True)
            az_own[w, 0:1, :] = jnp.sum(m32[0], axis=0, keepdims=True)
            az_own[w, 1:2, :] = cohesion
            for t in range(R - 1, -1, -1):
                for u in range(C - 1, -1, -1):
                    if t or u:
                        i = t * C + u
                        self.shares[i] = send(
                            az_own.at[w], az_in.at[w, i], az_s.at[w, i], az_r.at[w, i],
                            row_peer(t), flip(c, u, C),
                        )
            return own

        def attraction(self, own):
            w = self.w
            total = own + psum[w, 0]
            for s in range(1, Q):
                self.scatter[s].wait_recv()
                total = total + rin[w, s]
            for f in fulls:
                self.out[f].wait_recv()
                total = total + cr[w, f - 1]
            if has_half:
                @pl.when(is_guest)
                def _():
                    self.block_copy(half).wait_recv()
                    hz[...] = cr[w, half - 1]
                total = total + hz[...]
            return total

        def scales(self):
            w = self.w
            for i in self.shares:
                self.shares[i].wait_recv()
            az_in[w, 0] = az_own[w]
            both = jnp.sum(az_in[w], axis=0)
            inverse = 1.0 / both[0:1, :]
            return inverse, (both[1:2, :] * inverse) * (0.5 * inverse)

    def logits_of(attraction, scales):
        inverse, shift = scales
        logits = (attraction * inverse - shift) * (-1.0 / ANNEAL_TEMP_VALUE)
        return logits - jnp.max(logits, axis=1, keepdims=True)

    def member_of(attraction, scales):
        top = jnp.exp(logits_of(attraction, scales))
        return top * (1.0 / jnp.sum(top, axis=1, keepdims=True))

    own_e.wait()
    own_s.wait()
    ready_block(0, e_row[mine, :], seeds_to_member(s_row[b]))
    hear(e_direct[0])
    ready_rows(0)
    tile(0, 0)
    relays = {s: e_relay(s) for s in range(1, last)}
    if has_half:
        @pl.when(is_host)
        def _():
            hear(e_half)
            ready_guest(half)
            tile(half, 0)
    for s in range(1, last):
        hear(relays[s])
        ready_rows(s)
        tile(0, s)
        if has_half:
            @pl.when(is_host)
            def _():
                tile(half, s)
    early[0] = block_of(0, 0, 0, last)
    if has_half:
        @pl.when(is_host)
        def _():
            early[half] = block_of(0, half, 0, last)
            for s in range(last):
                hrow[s] = rows_of(0, half, s)
    relays[last] = e_relay(last)
    sweep = Sweep(0)
    for f in fulls:
        hear(e_guest[f])
        ready_guest(f)
    for s in range(last):
        for f in fulls:
            tile(f, s)
        sweep.rows(s)
    for f in fulls:
        early[f] = block_of(0, f, 0, last)
    hear(relays[last])
    ready_rows(last)
    for f in fulls:
        tile(f, last)
    if has_half:
        @pl.when(is_host)
        def _():
            tile(half, last)
            hrow[last] = rows_of(0, half, last)
    sweep.rows(last)
    for s in range(1, last):
        sweep.combine(s)
    cohesion = sweep.blocks()
    sweep.combine(last)
    sweep.combine(0)
    tile(0, last)
    own = sweep.share(cohesion)
    attraction = sweep.attraction(own)

    a_own[...] = attraction
    a_direct, a_guest, a_half = spread(
        (a_own,),
        (lambda s: a_row.at[row_slot(s, b)],),
        (lambda f: a_blk.at[f],),
        (ad_s,), (ad_r,), (ab_s,), (ab_r,),
    )

    def a_relay(s):
        hear(a_direct[s])
        at = row_slot(s, b)
        return [send(a_row.at[at], a_row.at[at], ar_s.at[s], ar_r.at[s], r, partner)]

    scales = sweep.scales()
    sweep = Sweep(1)

    def fill_rows(s, core, member):
        p1, p2 = split2(member)
        mp[row_slot(s, core), :k] = p1
        mp[row_slot(s, core), k:] = p2

    def fill_block(t):
        member = member_of(a_blk[t - 1], scales)
        p1, p2 = split2(member)
        m32[t] = member
        mf[t - 1, :n, :k] = p1
        mf[t - 1, :n, k:] = p2
        mf[t - 1, n:, :k] = p1
        mf[t - 1, n:, k:] = jnp.zeros_like(p1)

    own_member = member_of(attraction, scales)
    m32[0] = own_member
    fill_rows(0, b, own_member)
    hear(a_direct[0])
    fill_rows(0, 1 - b, member_of(a_row[row_slot(0, 1 - b), :], scales))
    relays = {}
    for s in range(1, last):
        relays[s] = a_relay(s)
        fill_rows(s, b, member_of(a_row[row_slot(s, b), :], scales))
    for s in range(1, last):
        hear(relays[s])
        fill_rows(s, 1 - b, member_of(a_row[row_slot(s, 1 - b), :], scales))
    if last:
        relays[last] = a_relay(last)
        fill_rows(last, b, member_of(a_row[row_slot(last, b), :], scales))
    early[0] = block_of(1, 0, 0, last)
    if has_half:
        @pl.when(is_host)
        def _():
            hear(a_half)
            fill_block(half)
            early[half] = block_of(1, half, 0, last)
            for s in range(Q):
                hrow[s] = rows_of(1, half, s)
    for f in fulls:
        hear(a_guest[f])
        fill_block(f)
    for s in list(range(1, Q)) + [0]:
        sweep.rows(s)
    for f in fulls:
        early[f] = block_of(1, f, 0, last)
    for s in range(1, Q):
        sweep.combine(s)
    hear(relays[last])
    fill_rows(last, 1 - b, member_of(a_row[row_slot(last, 1 - b), :], scales))
    cohesion = sweep.blocks()
    own = sweep.share(cohesion)
    sweep.combine(0)
    attraction = sweep.attraction(own)
    logits = logits_of(attraction, sweep.scales())
    o_ref[...] = logits - jnp.log(jnp.sum(jnp.exp(logits), axis=1, keepdims=True))

    for copy in started:
        copy.wait_send()
    if has_half:
        @pl.when(is_guest)
        def _():
            for copy in e_half + a_half:
                copy.wait_send()

        @pl.when(is_host)
        def _():
            for w in range(SWEEPS):
                Sweep(w).block_copy(half).wait_send()


def shards(R, C, embedding, seed_cluster):
    n, features = embedding.shape
    k = CLUSTER_COUNT
    Q = C // 2
    B = 1 + (R - 1) // 2 + (R % 2 == 0)
    G = max(B - 1, 1)
    dma = pltpu.SemaphoreType.DMA
    V = pltpu.VMEM
    W = SWEEPS
    return pl.pallas_call(
        functools.partial(kernel, R, C),
        out_shape=jax.ShapeDtypeStruct((n, k), F32),
        in_specs=[pl.BlockSpec(memory_space=pl.ANY)] * 2,
        out_specs=pl.BlockSpec(memory_space=pltpu.VMEM),
        scratch_shapes=[
            V((C * n, features), F32), V((C, 1, n), I32), V((G, n, features), F32), V((G, 1, n), I32),
            V((C * n, features), BF16), V((C * n, features), BF16), V((C * n, 1), F32),
            V((B, 2 * n, features), BF16), V((B, 8, n), F32), V((B, C * n, 2 * n), BF16),
            V((C * n, 2 * k), BF16), V((G, 2 * n, 2 * k), BF16), V((B, n, k), F32), V((B, n, k), F32),
            V((Q, 2 * n, k), F32), V((n, k), F32), V((1, k), F32),
            V((W, G, n, k), F32), V((W, G, n, k), F32),
            V((W, Q, 2, n, k), F32), V((W, Q, n, k), F32), V((W, Q, n, k), F32), V((W, Q, n, k), F32),
            V((n, k), F32), V((C * n, k), F32), V((G, n, k), F32),
            V((W, 2, k), F32), V((W, R * C, 2, k), F32),
            dma((2,)), dma((Q,)), dma((Q,)), dma((Q,)), dma((Q,)), dma((G,)), dma((G,)),
            dma((Q,)), dma((Q,)), dma((Q,)), dma((Q,)), dma((G,)), dma((G,)),
            dma((W, G)), dma((W, G)), dma((W, Q)), dma((W, Q)), dma((W, Q)), dma((W, Q)),
            dma((W, R * C)), dma((W, R * C)),
            dma((Q,)), dma((Q,)), dma((Q,)), dma((Q,)), dma((G,)), dma((G,)),
        ],
        compiler_params=pltpu.CompilerParams(
            collective_id=0, has_side_effects=True, vmem_limit_bytes=60 * 1024 * 1024
        ),
    )(embedding, seed_cluster.reshape(1, n))


def solution(mesh):
    return jax.shard_map(
        functools.partial(shards, mesh.shape["row"], mesh.shape["col"]),
        mesh=mesh,
        in_specs=(P(("row", "col"), None), P(("row", "col"))),
        out_specs=P(("row", "col"), None),
        check_vma=False,
    )
```

```python
import functools

import jax
import jax.numpy as jnp
from jax import lax
from jax.experimental import pallas as pl
from jax.experimental.pallas import tpu as pltpu
from jax.sharding import PartitionSpec as P

CLUSTER_COUNT = 128
SWEEPS = 2
ANNEAL_TEMP_VALUE = 0.02
MESH = pl.DeviceIdType.MESH
F32, BF16, I32 = jnp.float32, jnp.bfloat16, jnp.int32


def plane_order(R):
    return [2, 0, 3, 1] if R == 4 else list(range(R))


def flip(index, offset, size):
    out, bit = 0, 1
    while bit < size:
        out = out + bit * ((index // bit + offset // bit) % 2)
        bit *= 2
    return out


def look_up(index, values):
    out = jnp.int32(values[0])
    for i, value in enumerate(values):
        if i:
            out = jnp.where(index == i, jnp.int32(value), out)
    return out


def split2(x):
    first = x.astype(BF16)
    return first, (x - first.astype(F32)).astype(BF16)


def nt(a, b):
    return lax.dot_general(a, b, (((1,), (1,)), ((), ())), preferred_element_type=F32)


def tn(a, b):
    return lax.dot_general(a, b, (((0,), (0,)), ((), ())), preferred_element_type=F32)


def nn(a, b):
    return jnp.dot(a, b, preferred_element_type=F32)


def seeds_to_member(seeds):
    points = seeds.shape[1]
    labels = lax.broadcasted_iota(I32, (CLUSTER_COUNT, points), 0)
    chosen = jnp.where(labels == seeds, 0.5, 0.0).astype(F32)
    return chosen.T + 0.5 / CLUSTER_COUNT


def kernel(
    R, C, e_hbm, s_hbm, o_ref,
    e_row, s_row, e_grp, s_grp, eh, rsq, xh, xl, csq, dhl, ma, ma32, mb,
    r0, early, psum, rin, cc, ci, cs, cr, hz, a_own, a_row, a_grp, az_own, az_in,
    in_sem, ed_s, ed_r, eg_s, eg_r, el_s, el_r, sd_s, sd_r, sg_s, sg_r, sl_s, sl_r,
    cx_s, cx_r, cz_s, cz_r, rs_s, rs_r, az_s, az_r, ad_s, ad_r, ag_s, ag_r, al_s, al_r,
):
    n = e_hbm.shape[0]
    k = CLUSTER_COUNT
    Q = C // 2
    full = (R - 1) // 2
    has_half = R % 2 == 0
    half = 1 + full
    r = lax.axis_index("row")
    c = lax.axis_index("col")
    q, b = c // 2, c % 2
    order = plane_order(R)
    place = [order.index(i) for i in range(R)]
    guest_of = {f: look_up(r, [order[(place[i] + f) % R] for i in range(R)]) for f in range(1, half + 1)}
    host_of = {f: look_up(r, [order[(place[i] - f) % R] for i in range(R)]) for f in range(1, half + 1)}
    host_flag = look_up(r, [int(place[i] < R // 2) for i in range(R)])
    is_host = host_flag == 1
    is_guest = host_flag == 0
    fulls = list(range(1, full + 1))
    guests = fulls + ([half] if has_half else [])
    groups = [0] + guests
    last = Q - 1
    near = list(range(1, last))
    far = list(range(last, 0, -1))
    offsets = sorted(range(Q), key=lambda s: bin(s).count("1"))
    partner = q * 2 + (1 - b)
    started = []

    def remote(src, dst, ssem, rsem, row, col):
        return pltpu.make_async_remote_copy(
            src_ref=src, dst_ref=dst, send_sem=ssem, recv_sem=rsem,
            device_id=(row, col), device_id_type=MESH,
        )

    def start(copies):
        for copy in copies:
            copy.start()
            started.append(copy)
        return copies

    def hear(copies):
        for copy in copies:
            copy.wait_recv()

    def row_peer(t):
        return flip(r, t, R)

    def chip_peer(s):
        return flip(q, offsets[s], Q) * 2 + b

    def slot(s, count=1):
        return pl.ds(s * n, count * n)

    barrier = pltpu.get_barrier_semaphore()
    for s in range(1, Q):
        pl.semaphore_signal(barrier, inc=1, device_id=(r, chip_peer(s)), device_id_type=MESH)
    pl.semaphore_signal(barrier, inc=1, device_id=(r, partner), device_id_type=MESH)
    for t in range(1, R):
        pl.semaphore_signal(barrier, inc=1, device_id=(row_peer(t), c), device_id_type=MESH)
    own = [
        pltpu.make_async_copy(e_hbm, e_row.at[slot(0)], in_sem.at[0]),
        pltpu.make_async_copy(s_hbm, s_row.at[0], in_sem.at[1]),
        pltpu.make_async_copy(e_hbm, e_grp.at[0, b], in_sem.at[2]),
        pltpu.make_async_copy(s_hbm, s_grp.at[0, b], in_sem.at[3]),
    ]
    for copy in own:
        copy.start()
    if has_half:
        @pl.when(is_guest)
        def _():
            e_grp[half] = jnp.zeros(e_grp.shape[1:], F32)
            s_grp[half] = jnp.zeros(s_grp.shape[1:], I32)
            a_grp[half] = jnp.zeros(a_grp.shape[1:], F32)

        hz[...] = jnp.zeros_like(hz)
    pl.semaphore_wait(barrier, Q + R - 1)

    class Spread:
        def __init__(self, srcs, rows, grps, d_s, d_r, g_s, g_r, l_s, l_r, chips):
            self.grps, self.l_s, self.l_r = grps, l_s, l_r
            self.guest = {
                t: [
                    remote(src, grp.at[t, b], ss.at[t - 1], rs.at[t - 1], host_of[t], c)
                    for src, grp, ss, rs in zip(srcs, grps, g_s, g_r)
                ]
                for t in guests
            }
            self.direct = {
                s: [
                    remote(
                        src, row(s) if s else grp.at[0, b], ss.at[s], rs.at[s],
                        r, chip_peer(s) if s else partner,
                    )
                    for src, row, grp, ss, rs in zip(srcs, rows, grps, d_s, d_r)
                ]
                for s in range(Q)
            }
            for f in fulls:
                start(self.guest[f])
            start(self.direct[0])
            if has_half:
                @pl.when(is_guest)
                def _():
                    for copy in self.guest[half]:
                        copy.start()

            for s in chips:
                start(self.direct[s])

        def relay(self, t):
            return [
                remote(grp.at[t, b], grp.at[t, b], ss.at[t - 1], rs.at[t - 1], r, partner)
                for grp, ss, rs in zip(self.grps, self.l_s, self.l_r)
            ]

        def pass_on(self, t):
            hear(self.guest[t])
            for copy in self.relay(t):
                copy.start()

        def pass_half(self):
            if has_half:
                @pl.when(is_host)
                def _():
                    self.pass_on(half)

        def hear_half(self):
            if has_half:
                @pl.when(is_host)
                def _():
                    hear(self.relay(half))

        def finish(self):
            for f in fulls:
                for copy in self.relay(f):
                    copy.wait_send()
            if has_half:
                @pl.when(is_guest)
                def _():
                    for copy in self.guest[half]:
                        copy.wait_send()

                @pl.when(is_host)
                def _():
                    for copy in self.relay(half):
                        copy.wait_send()

    points = Spread(
        (s_hbm, e_hbm), (lambda s: s_row.at[s], lambda s: e_row.at[slot(s)]), (s_grp, e_grp),
        (sd_s, ed_s), (sd_r, ed_r), (sg_s, eg_s), (sg_r, eg_r), (sl_s, el_s), (sl_r, el_r), range(1, Q),
    )

    def masked(t, member):
        return jnp.where(is_host, member, 0.0) if has_half and t == half else member

    def put_group(w, t, core, member):
        p1, p2 = split2(masked(t, member))
        for low in range(2):
            at = slot(4 * t + 2 * low + core)
            mb[at, :k] = p1
            if w:
                mb[at, k:] = jnp.zeros_like(p2) if low else p2

    def put_rows(w, s, member):
        p1, p2 = split2(member)
        ma32[slot(s), :] = member
        ma[slot(s), :k] = p1
        if w:
            ma[slot(s), k:] = p2

    def ready_group(t):
        x = e_grp[t].reshape(2 * n, e_hbm.shape[1])
        p1, p2 = split2(-2.0 * x)
        xh[t] = p1
        xl[t] = p2
        q1, q2 = split2(x * x)
        ones = jnp.ones((8, x.shape[1]), BF16)
        csq[t] = nt(ones, q2) + nt(ones, q1) + 1.0
        for core in range(2):
            put_group(0, t, core, seeds_to_member(s_grp[t, core]))

    def ready_rows(s):
        x = e_row[slot(s), :]
        p1, p2 = split2(x)
        eh[s, :n, :] = p1
        eh[s, n:, :] = p2
        rsq[s] = jnp.sum(x * x, axis=1, keepdims=True)
        put_rows(0, s, seeds_to_member(s_row[s]))

    def tile(t, s):
        both = nt(eh[s], xh[t])
        inner = both[:n] + (both[n:] + nt(eh[s, :n, :], xl[t]))
        p1, p2 = split2(jnp.sqrt(rsq[s] + csq[t, 0:1, :] + inner))
        dhl[slot(s), slot(4 * t, 2)] = p1
        dhl[slot(s), slot(4 * t + 2, 2)] = p2

    def rows_of(w, t0, t1, s0, s1):
        d = dhl[slot(s0, s1 - s0), slot(4 * t0, 4 * (t1 - t0))]
        m = slot(4 * t0, 4 * (t1 - t0))
        if w == 0:
            return nn(d, mb[m, :k])
        both = nn(d, mb[m, :])
        return both[:, :k] + both[:, k:]

    def group_of(w, t, s0, s1):
        d = dhl[slot(s0, s1 - s0), slot(4 * t, 4)]
        if w == 0:
            both = tn(d, ma[slot(s0, s1 - s0), :k])
            return both[: 2 * n] + both[2 * n :]
        both = tn(d, ma[slot(s0, s1 - s0), :])
        return both[: 2 * n, :k] + (both[2 * n :, :k] + both[: 2 * n, k:])

    class Sweep:
        def __init__(self, w):
            self.w, self.scatter, self.shares, self.parts = w, {}, {}, []

        def rows(self, s, own_part):
            w = self.w
            guest_part = rows_of(w, 1, len(groups), s, s + 1)
            part = own_part + guest_part
            psum[w, s] = part
            if s:
                self.scatter[s] = start([
                    remote(psum.at[w, s], rin.at[w, s], rs_s.at[w, s], rs_r.at[w, s], r, chip_peer(s))
                ])
            self.parts.append(jnp.sum(ma32[slot(s), :] * (part + guest_part), axis=0, keepdims=True))

        def cross(self, t):
            w = self.w
            return remote(cc.at[w, t - 1, 1 - b], ci.at[w, t - 1], cx_s.at[w, t - 1], cx_r.at[w, t - 1], r, partner)

        def away(self, t):
            w = self.w
            return remote(cs.at[w, t - 1], cr.at[w, t - 1], cz_s.at[w, t - 1], cz_r.at[w, t - 1], guest_of[t], c)

        def group(self, t, part):
            w = self.w
            cc[w, t - 1, 0] = part[:n]
            cc[w, t - 1, 1] = part[n:]
            start([self.cross(t)])

        def send_groups(self):
            w = self.w
            for t in guests:
                self.cross(t).wait_recv()
                cs[w, t - 1] = cc[w, t - 1, b] + ci[w, t - 1]
                if t in fulls:
                    start([self.away(t)])
                else:
                    @pl.when(is_host)
                    def _():
                        self.away(t).start()

        def share(self):
            w = self.w
            cohesion = self.parts[0]
            for part in self.parts[1:]:
                cohesion = cohesion + part
            az_own[w, 0:1, :] = jnp.sum(ma32[slot(0), :], axis=0, keepdims=True)
            az_own[w, 1:2, :] = cohesion
            for t in range(R - 1, -1, -1):
                for u in range(C - 1, -1, -1):
                    if t or u:
                        i = t * C + u
                        self.shares[i] = start([
                            remote(
                                az_own.at[w], az_in.at[w, i], az_s.at[w, i], az_r.at[w, i],
                                row_peer(t), flip(c, u, C),
                            )
                        ])

        def attraction(self):
            w = self.w
            total = psum[w, 0]
            for s in far:
                hear(self.scatter[s])
                total = total + rin[w, s]
            for f in fulls:
                self.away(f).wait_recv()
                total = total + cr[w, f - 1]
            if has_half:
                @pl.when(is_guest)
                def _():
                    self.away(half).wait_recv()
                    hz[...] = cr[w, half - 1]
                total = total + hz[...]
            return total

        def scales(self):
            w = self.w
            for i in self.shares:
                hear(self.shares[i])
            az_in[w, 0] = az_own[w]
            both = jnp.sum(az_in[w], axis=0)
            inverse = 1.0 / both[0:1, :]
            return inverse, (both[1:2, :] * inverse) * (0.5 * inverse)

        def finish(self):
            if has_half:
                @pl.when(is_host)
                def _():
                    self.away(half).wait_send()

    def logits_of(attraction, scales):
        inverse, shift = scales
        logits = (attraction * inverse - shift) * (-1.0 / ANNEAL_TEMP_VALUE)
        return logits - jnp.max(logits, axis=1, keepdims=True)

    def member_of(attraction, scales):
        top = jnp.exp(logits_of(attraction, scales))
        return top * (1.0 / jnp.sum(top, axis=1, keepdims=True))

    sweep = Sweep(0)
    for copy in own:
        copy.wait()
    ready_rows(0)
    hear(points.direct[0])
    ready_group(0)
    tile(0, 0)
    for s in near:
        hear(points.direct[s])
        ready_rows(s)
        tile(0, s)
    for f in fulls:
        points.pass_on(f)
    for f in fulls:
        hear(points.relay(f))
        ready_group(f)
    points.pass_half()
    for f in fulls:
        for s in range(last):
            tile(f, s)
    points.hear_half()
    if has_half:
        ready_group(half)
        for s in range(last):
            tile(half, s)
    for s in near + [0]:
        sweep.rows(s, rows_of(0, 0, 1, s, s + 1))
    for t in guests:
        early[t - 1] = group_of(0, t, 0, last)
    hear(points.direct[last])
    ready_rows(last)
    for t in groups:
        tile(t, last)
    for t in guests:
        sweep.group(t, early[t - 1] + group_of(0, t, last, Q))
    sweep.rows(last, rows_of(0, 0, 1, last, Q))
    sweep.send_groups()
    sweep.share()
    attraction = sweep.attraction()

    a_own[...] = attraction
    sums = Spread(
        (a_own,), (lambda s: a_row.at[slot(s)],), (a_grp,),
        (ad_s,), (ad_r,), (ag_s,), (ag_r,), (al_s,), (al_r,), far,
    )
    scales = sweep.scales()
    first, sweep = sweep, Sweep(1)
    own_member = member_of(attraction, scales)
    put_rows(1, 0, own_member)
    a_grp[0, b] = attraction
    hear(sums.direct[0])
    for core in range(2):
        put_group(1, 0, core, member_of(a_grp[0, core], scales))
    r0[...] = rows_of(1, 0, 1, 0, Q)
    for f in fulls:
        sums.pass_on(f)
    for s in far:
        hear(sums.direct[s])
        put_rows(1, s, member_of(a_row[slot(s), :], scales))
    sums.pass_half()
    for t in guests:
        sweep.group(t, group_of(1, t, 0, Q))
    for f in fulls:
        hear(sums.relay(f))
        for core in range(2):
            put_group(1, f, core, member_of(a_grp[f, core], scales))
    sums.hear_half()
    if has_half:
        for core in range(2):
            put_group(1, half, core, member_of(a_grp[half, core], scales))
    for s in far + [0]:
        sweep.rows(s, r0[slot(s), :])
    sweep.send_groups()
    sweep.share()
    attraction = sweep.attraction()
    logits = logits_of(attraction, sweep.scales())
    o_ref[...] = logits - jnp.log(jnp.sum(jnp.exp(logits), axis=1, keepdims=True))

    for copy in started:
        copy.wait_send()
    for part in (points, sums, first, sweep):
        part.finish()


def shards(R, C, embedding, seed_cluster):
    n, features = embedding.shape
    k = CLUSTER_COUNT
    Q = C // 2
    B = 1 + (R - 1) // 2 + (R % 2 == 0)
    G = max(B - 1, 1)
    dma = pltpu.SemaphoreType.DMA
    V = pltpu.VMEM
    W = SWEEPS
    return pl.pallas_call(
        functools.partial(kernel, R, C),
        out_shape=jax.ShapeDtypeStruct((n, k), F32),
        in_specs=[pl.BlockSpec(memory_space=pl.ANY)] * 2,
        out_specs=pl.BlockSpec(memory_space=pltpu.VMEM),
        scratch_shapes=[
            V((Q * n, features), F32), V((Q, 1, n), I32), V((B, 2, n, features), F32), V((B, 2, 1, n), I32),
            V((Q, 2 * n, features), BF16), V((Q, n, 1), F32),
            V((B, 2 * n, features), BF16), V((B, 2 * n, features), BF16), V((B, 8, 2 * n), F32),
            V((Q * n, B * 4 * n), BF16), V((Q * n, 2 * k), BF16), V((Q * n, k), F32), V((B * 4 * n, 2 * k), BF16),
            V((Q * n, k), F32), V((G, 2 * n, k), F32),
            V((W, Q, n, k), F32), V((W, Q, n, k), F32), V((W, G, 2, n, k), F32),
            V((W, G, n, k), F32), V((W, G, n, k), F32), V((W, G, n, k), F32), V((n, k), F32),
            V((n, k), F32), V((Q * n, k), F32), V((B, 2, n, k), F32),
            V((W, 2, k), F32), V((W, R * C, 2, k), F32),
            dma((4,)), dma((Q,)), dma((Q,)), dma((G,)), dma((G,)), dma((G,)), dma((G,)),
            dma((Q,)), dma((Q,)), dma((G,)), dma((G,)), dma((G,)), dma((G,)),
            dma((W, G)), dma((W, G)), dma((W, G)), dma((W, G)), dma((W, Q)), dma((W, Q)),
            dma((W, R * C)), dma((W, R * C)),
            dma((Q,)), dma((Q,)), dma((G,)), dma((G,)), dma((G,)), dma((G,)),
        ],
        compiler_params=pltpu.CompilerParams(
            collective_id=0, has_side_effects=True, vmem_limit_bytes=56426496
        ),
    )(embedding, seed_cluster.reshape(1, n))


def solution(mesh):
    return jax.shard_map(
        functools.partial(shards, mesh.shape["row"], mesh.shape["col"]),
        mesh=mesh,
        in_specs=(P(("row", "col"), None), P(("row", "col"))),
        out_specs=P(("row", "col"), None),
        check_vma=False,
    )
```

```python
import functools

import jax
import jax.numpy as jnp
from jax import lax
from jax.experimental import pallas as pl
from jax.experimental.pallas import tpu as pltpu
from jax.sharding import PartitionSpec as P

CLUSTER_COUNT = 128
SWEEPS = 2
ANNEAL_TEMP_VALUE = 0.02
MESH = pl.DeviceIdType.MESH
F32, BF16, I32 = jnp.float32, jnp.bfloat16, jnp.int32


def plane_order(R):
    return [2, 0, 3, 1] if R == 4 else list(range(R))


def flip(index, offset, size):
    out, bit = 0, 1
    while bit < size:
        out = out + bit * ((index // bit + offset // bit) % 2)
        bit *= 2
    return out


def look_up(index, values):
    out = jnp.int32(values[0])
    for i, value in enumerate(values):
        if i:
            out = jnp.where(index == i, jnp.int32(value), out)
    return out


def split2(x):
    first = x.astype(BF16)
    return first, (x - first.astype(F32)).astype(BF16)


def nt(a, b):
    return lax.dot_general(a, b, (((1,), (1,)), ((), ())), preferred_element_type=F32)


def tn(a, b):
    return lax.dot_general(a, b, (((0,), (0,)), ((), ())), preferred_element_type=F32)


def nn(a, b):
    return jnp.dot(a, b, preferred_element_type=F32)


def seeds_to_member(seeds):
    points = seeds.shape[1]
    labels = lax.broadcasted_iota(I32, (CLUSTER_COUNT, points), 0)
    chosen = jnp.where(labels == seeds, 0.5, 0.0).astype(F32)
    return chosen.T + 0.5 / CLUSTER_COUNT


def kernel(
    R, C, e_hbm, s_hbm, o_ref,
    e_row, s_row, e_grp, s_grp, eh, rsq, xh, xl, csq, dhl, ma, ma32, mb,
    r0, r1, early, psum, rin, cc, ci, cs, cr, hz, a_own, a_row, a_grp, az_own, az_in,
    in_sem, ed_s, ed_r, eg_s, eg_r, el_s, el_r, sd_s, sd_r, sg_s, sg_r, sl_s, sl_r,
    cx_s, cx_r, cz_s, cz_r, rs_s, rs_r, az_s, az_r, ad_s, ad_r, ag_s, ag_r, al_s, al_r,
):
    n = e_hbm.shape[0]
    k = CLUSTER_COUNT
    Q = C // 2
    full = (R - 1) // 2
    has_half = R % 2 == 0
    half = 1 + full
    r = lax.axis_index("row")
    c = lax.axis_index("col")
    q, b = c // 2, c % 2
    order = plane_order(R)
    place = [order.index(i) for i in range(R)]
    guest_of = {f: look_up(r, [order[(place[i] + f) % R] for i in range(R)]) for f in range(1, half + 1)}
    host_of = {f: look_up(r, [order[(place[i] - f) % R] for i in range(R)]) for f in range(1, half + 1)}
    host_flag = look_up(r, [int(place[i] < R // 2) for i in range(R)])
    is_host = host_flag == 1
    is_guest = host_flag == 0
    fulls = list(range(1, full + 1))
    guests = fulls + ([half] if has_half else [])
    groups = [0] + guests
    last = Q - 1
    near = list(range(1, last))
    far = list(range(last, 0, -1))
    offsets = sorted(range(Q), key=lambda s: bin(s).count("1"))
    started = []

    def remote(src, dst, ssem, rsem, row, col):
        return pltpu.make_async_remote_copy(
            src_ref=src, dst_ref=dst, send_sem=ssem, recv_sem=rsem,
            device_id=(row, col), device_id_type=MESH,
        )

    def start(copies):
        for copy in copies:
            copy.start()
            started.append(copy)
        return copies

    def hear(copies):
        for copy in copies:
            copy.wait_recv()

    row_peers = [flip(r, t, R) for t in range(R)]
    col_peers = [flip(c, u, C) for u in range(C)]

    partner = col_peers[1]

    def chip_peer(s):
        return col_peers[2 * offsets[s]]

    def slot(s, count=1):
        return pl.ds(s * n, count * n)

    barrier = pltpu.get_barrier_semaphore()
    for s in range(1, Q):
        pl.semaphore_signal(barrier, inc=1, device_id=(r, chip_peer(s)), device_id_type=MESH)
    pl.semaphore_signal(barrier, inc=1, device_id=(r, partner), device_id_type=MESH)
    for f in fulls:
        pl.semaphore_signal(barrier, inc=1, device_id=(guest_of[f], c), device_id_type=MESH)
    if has_half:
        @pl.when(is_host)
        def _():
            pl.semaphore_signal(barrier, inc=1, device_id=(guest_of[half], c), device_id_type=MESH)

    own = [
        pltpu.make_async_copy(e_hbm, e_row.at[slot(0)], in_sem.at[0]),
        pltpu.make_async_copy(s_hbm, s_row.at[0], in_sem.at[1]),
        pltpu.make_async_copy(e_hbm, e_grp.at[0, 0], in_sem.at[2]),
        pltpu.make_async_copy(s_hbm, s_grp.at[0, 0], in_sem.at[3]),
    ]
    for copy in own:
        copy.start()
    if has_half:
        @pl.when(is_guest)
        def _():
            for core in range(2):
                e_grp[core, half] = jnp.zeros(e_grp.shape[2:], F32)
                s_grp[core, half] = jnp.zeros(s_grp.shape[2:], I32)
                a_grp[core, half] = jnp.zeros(a_grp.shape[2:], F32)

        hz[...] = jnp.zeros_like(hz)
    pl.semaphore_wait(barrier, Q + full + (1 - host_flag if has_half else 0))

    class Spread:
        def __init__(self, srcs, rows, grps, d_s, d_r, g_s, g_r, l_s, l_r, chips):
            self.grps, self.l_s, self.l_r = grps, l_s, l_r
            self.guest = {
                t: [
                    remote(src, grp.at[0, t], ss.at[t - 1], rs.at[t - 1], host_of[t], c)
                    for src, grp, ss, rs in zip(srcs, grps, g_s, g_r)
                ]
                for t in guests
            }
            self.direct = {
                s: [
                    remote(
                        src, row(s) if s else grp.at[1, 0], ss.at[s], rs.at[s],
                        r, chip_peer(s) if s else partner,
                    )
                    for src, row, grp, ss, rs in zip(srcs, rows, grps, d_s, d_r)
                ]
                for s in range(Q)
            }
            for f in fulls:
                start(self.guest[f])
            start(self.direct[0])
            if has_half:
                @pl.when(is_guest)
                def _():
                    for copy in self.guest[half]:
                        copy.start()

            for s in chips:
                start(self.direct[s])

        def relay(self, t):
            return [
                remote(grp.at[0, t], grp.at[1, t], ss.at[t - 1], rs.at[t - 1], r, partner)
                for grp, ss, rs in zip(self.grps, self.l_s, self.l_r)
            ]

        def pass_on(self, t):
            hear(self.guest[t])
            for copy in self.relay(t):
                copy.start()

        def pass_half(self):
            if has_half:
                @pl.when(is_host)
                def _():
                    self.pass_on(half)

        def hear_half(self):
            if has_half:
                @pl.when(is_host)
                def _():
                    hear(self.relay(half))

        def finish(self):
            for f in fulls:
                for copy in self.relay(f):
                    copy.wait_send()
            if has_half:
                @pl.when(is_guest)
                def _():
                    for copy in self.guest[half]:
                        copy.wait_send()

                @pl.when(is_host)
                def _():
                    for copy in self.relay(half):
                        copy.wait_send()

    points = Spread(
        (s_hbm, e_hbm), (lambda s: s_row.at[s], lambda s: e_row.at[slot(s)]), (s_grp, e_grp),
        (sd_s, ed_s), (sd_r, ed_r), (sg_s, eg_s), (sg_r, eg_r), (sl_s, el_s), (sl_r, el_r), range(1, Q),
    )

    B = len(groups)

    def span(core, t0, t1, width=1):
        return slot((core * B + t0) * width, (t1 - t0) * width)

    def put_group(w, core, t, member):
        if has_half and t == half:
            member = jnp.where(is_host, member, 0.0)
        p1, p2 = split2(member)
        for low in range(2):
            at = slot((core * B + t) * 2 + low)
            mb[at, :k] = p1
            if w:
                mb[at, k:] = jnp.zeros_like(p2) if low else p2
        return member

    def put_rows(w, s, member):
        p1, p2 = split2(member)
        ma32[slot(s), :] = member
        ma[slot(s), :k] = p1
        if w:
            ma[slot(s), k:] = p2

    def ready_group(core, t):
        x = e_grp[core, t]
        p1, p2 = split2(-2.0 * x)
        at = span(core, t, t + 1)
        xh[at, :] = p1
        xl[at, :] = p2
        q1, q2 = split2(x * x)
        ones = jnp.ones((8, x.shape[1]), BF16)
        csq[:, at] = nt(ones, q2) + nt(ones, q1) + 1.0
        put_group(0, core, t, seeds_to_member(s_grp[core, t]))

    def ready_rows(s):
        x = e_row[slot(s), :]
        p1, p2 = split2(x)
        eh[s, :n, :] = p1
        eh[s, n:, :] = p2
        rsq[s] = jnp.sum(x * x, axis=1, keepdims=True)
        put_rows(0, s, seeds_to_member(s_row[s]))

    def tile(core, t0, t1, s):
        at = span(core, t0, t1)
        both = nt(eh[s], xh[at, :])
        inner = both[:n] + (both[n:] + nt(eh[s, :n, :], xl[at, :]))
        p1, p2 = split2(jnp.sqrt(rsq[s] + csq[0:1, at] + inner))
        for t in range(t0, t1):
            part = slice((t - t0) * n, (t - t0 + 1) * n)
            dhl[slot(s), slot((core * B + t) * 2)] = p1[:, part]
            dhl[slot(s), slot((core * B + t) * 2 + 1)] = p2[:, part]

    def rows_of(w, core, t0, t1, s0, s1):
        at = span(core, t0, t1, 2)
        d = dhl[slot(s0, s1 - s0), at]
        if w == 0:
            return nn(d, mb[at, :k])
        both = nn(d, mb[at, :])
        return both[:, :k] + both[:, k:]

    def groups_of(w, core, s0, s1):
        rows = slot(s0, s1 - s0)
        both = tn(dhl[rows, span(core, 1, B, 2)], ma[rows, :k] if w == 0 else ma[rows, :])
        if w:
            both = both[:, :k] + both[:, k:]
        return [both[2 * i * n : (2 * i + 1) * n] + both[(2 * i + 1) * n : (2 * i + 2) * n] for i in range(B - 1)]

    def over(member, sums):
        return jnp.sum(member * sums, axis=0, keepdims=True)

    class Sweep:
        def __init__(self, w):
            self.w, self.scatter, self.shares, self.parts = w, {}, {}, []

        def rows(self, s, own_part, guest_part):
            psum[self.w, s] = own_part + guest_part

        def send_rows(self, s):
            w = self.w
            self.scatter[s] = start([
                remote(psum.at[w, s], rin.at[w, s], rs_s.at[w, s], rs_r.at[w, s], r, chip_peer(s))
            ])

        def cross(self, t):
            w = self.w
            return remote(cc.at[w, t - 1], ci.at[w, t - 1], cx_s.at[w, t - 1], cx_r.at[w, t - 1], r, partner)

        def away(self, t):
            w = self.w
            return remote(cs.at[w, t - 1], cr.at[w, t - 1], cz_s.at[w, t - 1], cz_r.at[w, t - 1], guest_of[t], c)

        def cross_groups(self, parts):
            for t in guests:
                cc[self.w, t - 1] = parts[t - 1]
            for t in guests:
                start([self.cross(t)])

        def send_groups(self, parts):
            w = self.w
            for t in guests:
                self.cross(t).wait_recv()
                cs[w, t - 1] = parts[t - 1] + ci[w, t - 1]
                if t in fulls:
                    start([self.away(t)])
                else:
                    @pl.when(is_host)
                    def _():
                        self.away(t).start()

        def total(self):
            w = self.w
            cohesion = self.parts[0]
            for part in self.parts[1:]:
                cohesion = cohesion + part
            az_own[w, 0:1, :] = jnp.sum(ma32[slot(0), :], axis=0, keepdims=True)
            az_own[w, 1:2, :] = cohesion

        def share(self, us):
            w = self.w
            for t in range(R - 1, -1, -1):
                for u in us:
                    if t or u:
                        i = t * C + u
                        self.shares[i] = start([
                            remote(
                                az_own.at[w], az_in.at[w, i], az_s.at[w, i], az_r.at[w, i],
                                row_peers[t], col_peers[u],
                            )
                        ])

        def attraction(self):
            w = self.w
            total = psum[w, 0]
            for s in far:
                hear(self.scatter[s])
                total = total + rin[w, s]
            for f in fulls:
                self.away(f).wait_recv()
                total = total + cr[w, f - 1]
            if has_half:
                @pl.when(is_guest)
                def _():
                    self.away(half).wait_recv()
                    hz[...] = cr[w, half - 1]
                total = total + hz[...]
            return total

        def scales(self):
            w = self.w
            for i in self.shares:
                hear(self.shares[i])
            az_in[w, 0] = az_own[w]
            both = jnp.sum(az_in[w], axis=0)
            inverse = 1.0 / both[0:1, :]
            return inverse, (both[1:2, :] * inverse) * (0.5 * inverse)

        def finish(self):
            if has_half:
                @pl.when(is_host)
                def _():
                    self.away(half).wait_send()

    def logits_of(attraction, scales):
        inverse, shift = scales
        logits = (attraction * inverse - shift) * (-1.0 / ANNEAL_TEMP_VALUE)
        return logits - jnp.max(logits, axis=1, keepdims=True)

    def member_of(attraction, scales):
        top = jnp.exp(logits_of(attraction, scales))
        return top * (1.0 / jnp.sum(top, axis=1, keepdims=True))

    sweep = Sweep(0)
    for copy in own:
        copy.wait()
    ready_rows(0)
    ready_group(0, 0)
    tile(0, 0, 1, 0)
    hear(points.direct[0])
    ready_group(1, 0)
    tile(1, 0, 1, 0)
    for s in near:
        hear(points.direct[s])
        ready_rows(s)
        for core in range(2):
            tile(core, 0, 1, s)
    for f in fulls:
        points.pass_on(f)
        ready_group(0, f)
    for f in fulls:
        for s in range(last):
            tile(0, f, f + 1, s)
    points.pass_half()
    for f in fulls:
        hear(points.relay(f))
        ready_group(1, f)
    for f in fulls:
        for s in range(last):
            tile(1, f, f + 1, s)
    points.hear_half()
    if has_half:
        for core in range(2):
            ready_group(core, half)
            for s in range(last):
                tile(core, half, half + 1, s)
    both = rows_of(0, 0, 1, B, 0, last) + rows_of(0, 1, 1, B, 0, last)
    mine = rows_of(0, 0, 0, 1, 0, last) + rows_of(0, 1, 0, 1, 0, last)
    for s in range(last):
        own_part, guest_part = mine[s * n : (s + 1) * n], both[s * n : (s + 1) * n]
        sweep.rows(s, own_part, guest_part)
        sweep.parts.append(over(ma32[slot(s), :], own_part + 2.0 * guest_part))
    for s in near:
        sweep.send_rows(s)
    for core in range(2):
        for i, part in enumerate(groups_of(0, core, 0, last)):
            early[core, i] = part
    hear(points.direct[last])
    ready_rows(last)
    tile(1, 1, B, last)
    sweep.cross_groups([early[1, i] + part for i, part in enumerate(groups_of(0, 1, last, Q))])
    tile(0, 1, B, last)
    parts = [early[0, i] + part for i, part in enumerate(groups_of(0, 0, last, Q))]
    for core in range(2):
        tile(core, 0, 1, last)
    own_part = rows_of(0, 0, 0, 1, last, Q) + rows_of(0, 1, 0, 1, last, Q)
    guest_part = rows_of(0, 0, 1, B, last, Q) + rows_of(0, 1, 1, B, last, Q)
    sweep.rows(last, own_part, guest_part)
    sweep.parts.append(over(ma32[slot(last), :], own_part + 2.0 * guest_part))
    sweep.send_rows(last)
    sweep.send_groups(parts)
    sweep.total()
    sweep.share(range(C - 1, -1, -1))
    attraction = sweep.attraction()

    a_own[...] = attraction
    sums = Spread(
        (a_own,), (lambda s: a_row.at[slot(s)],), (a_grp,),
        (ad_s,), (ad_r,), (ag_s,), (ag_r,), (al_s,), (al_r,), far,
    )
    scales = sweep.scales()
    first, sweep = sweep, Sweep(1)
    own_member = member_of(attraction, scales)
    put_rows(1, 0, own_member)
    put_group(1, 0, 0, own_member)
    hear(sums.direct[0])
    put_group(1, 1, 0, member_of(a_grp[1, 0], scales))
    r0[...] = rows_of(1, 0, 0, 1, 0, Q) + rows_of(1, 1, 0, 1, 0, Q)
    sweep.parts.append(over(own_member, r0[slot(0), :]))
    for f in fulls:
        sums.pass_on(f)
    for s in far:
        hear(sums.direct[s])
        member = member_of(a_row[slot(s), :], scales)
        put_rows(1, s, member)
        sweep.parts.append(over(member, r0[slot(s), :]))
    cross = groups_of(1, 1, 0, Q)
    sweep.cross_groups(cross)
    sums.pass_half()
    parts = groups_of(1, 0, 0, Q)
    for t in guests:
        sweep.parts.append(over(put_group(1, 0, t, member_of(a_grp[0, t], scales)), 2.0 * parts[t - 1]))
    r1[...] = rows_of(1, 0, 1, B, 0, Q)
    for f in fulls:
        hear(sums.relay(f))
    sums.hear_half()
    for t in guests:
        sweep.parts.append(over(put_group(1, 1, t, member_of(a_grp[1, t], scales)), 2.0 * cross[t - 1]))
    sweep.total()
    sweep.share(range(C - 1, -1, -1))
    sweep.send_groups(parts)
    both = r1[...] + rows_of(1, 1, 1, B, 0, Q)
    for s in far + [0]:
        sweep.rows(s, r0[slot(s), :], both[s * n : (s + 1) * n])
        if s:
            sweep.send_rows(s)
    attraction = sweep.attraction()
    logits = logits_of(attraction, sweep.scales())
    o_ref[...] = logits - jnp.log(jnp.sum(jnp.exp(logits), axis=1, keepdims=True))

    for copy in started:
        copy.wait_send()
    for part in (points, sums, first, sweep):
        part.finish()


def shards(R, C, embedding, seed_cluster):
    n, features = embedding.shape
    k = CLUSTER_COUNT
    Q = C // 2
    B = 1 + (R - 1) // 2 + (R % 2 == 0)
    G = max(B - 1, 1)
    dma = pltpu.SemaphoreType.DMA
    V = pltpu.VMEM
    W = SWEEPS
    return pl.pallas_call(
        functools.partial(kernel, R, C),
        out_shape=jax.ShapeDtypeStruct((n, k), F32),
        in_specs=[pl.BlockSpec(memory_space=pl.ANY)] * 2,
        out_specs=pl.BlockSpec(memory_space=pltpu.VMEM),
        scratch_shapes=[
            V((Q * n, features), F32), V((Q, 1, n), I32), V((2, B, n, features), F32), V((2, B, 1, n), I32),
            V((Q, 2 * n, features), BF16), V((Q, n, 1), F32),
            V((2 * B * n, features), BF16), V((2 * B * n, features), BF16), V((8, 2 * B * n), F32),
            V((Q * n, B * 4 * n), BF16), V((Q * n, 2 * k), BF16), V((Q * n, k), F32), V((B * 4 * n, 2 * k), BF16),
            V((Q * n, k), F32), V((Q * n, k), F32), V((2, G, n, k), F32),
            V((W, Q, n, k), F32), V((W, Q, n, k), F32), V((W, G, n, k), F32),
            V((W, G, n, k), F32), V((W, G, n, k), F32), V((W, G, n, k), F32), V((n, k), F32),
            V((n, k), F32), V((Q * n, k), F32), V((2, B, n, k), F32),
            V((W, 2, k), F32), V((W, R * C, 2, k), F32),
            dma((4,)), dma((Q,)), dma((Q,)), dma((G,)), dma((G,)), dma((G,)), dma((G,)),
            dma((Q,)), dma((Q,)), dma((G,)), dma((G,)), dma((G,)), dma((G,)),
            dma((W, G)), dma((W, G)), dma((W, G)), dma((W, G)), dma((W, Q)), dma((W, Q)),
            dma((W, R * C)), dma((W, R * C)),
            dma((Q,)), dma((Q,)), dma((G,)), dma((G,)), dma((G,)), dma((G,)),
        ],
        compiler_params=pltpu.CompilerParams(
            collective_id=0, has_side_effects=True, vmem_limit_bytes=56426496
        ),
    )(embedding, seed_cluster.reshape(1, n))


def solution(mesh):
    return jax.shard_map(
        functools.partial(shards, mesh.shape["row"], mesh.shape["col"]),
        mesh=mesh,
        in_specs=(P(("row", "col"), None), P(("row", "col"))),
        out_specs=P(("row", "col"), None),
        check_vma=False,
    )
```

```python
import functools

import jax
import jax.numpy as jnp
from jax import lax
from jax.experimental import pallas as pl
from jax.experimental.pallas import tpu as pltpu
from jax.sharding import PartitionSpec as P

CLUSTER_COUNT = 128
SWEEPS = 2
PIECES = 1
ANNEAL_TEMP_VALUE = 0.02
MESH = pl.DeviceIdType.MESH
F32, BF16, I32 = jnp.float32, jnp.bfloat16, jnp.int32


def plane_order(R):
    return [2, 0, 3, 1] if R == 4 else list(range(R))


def flip(index, offset, size):
    out, bit = 0, 1
    while bit < size:
        out = out + bit * ((index // bit + offset // bit) % 2)
        bit *= 2
    return out


def look_up(index, values):
    out = jnp.int32(values[0])
    for i, value in enumerate(values):
        if i:
            out = jnp.where(index == i, jnp.int32(value), out)
    return out


def split2(x):
    first = x.astype(BF16)
    return first, (x - first.astype(F32)).astype(BF16)


def nt(a, b):
    return lax.dot_general(a, b, (((1,), (1,)), ((), ())), preferred_element_type=F32)


def tn(a, b):
    return lax.dot_general(a, b, (((0,), (0,)), ((), ())), preferred_element_type=F32)


def nn(a, b):
    return jnp.dot(a, b, preferred_element_type=F32)


def seeds_to_member(seeds):
    points = seeds.shape[1]
    labels = lax.broadcasted_iota(I32, (CLUSTER_COUNT, points), 0)
    chosen = jnp.where(labels == seeds, 0.5, 0.0).astype(F32)
    return chosen.T + 0.5 / CLUSTER_COUNT


def kernel(
    R, C, e_hbm, s_hbm, o_ref,
    e_row, s_row, e_grp, s_grp, eh, rsq, xh, xl, csq, dhl, ma, ma32, mb,
    r0, r1, psum, rin, cc, ci, cs, cr, hz, a_own, a_row, a_grp, az_own, az_in,
    in_sem, ed_s, ed_r, eg_s, eg_r, el_s, el_r, sd_s, sd_r, sg_s, sg_r, sl_s, sl_r,
    cx_s, cx_r, cz_s, cz_r, rs_s, rs_r, az_s, az_r, ad_s, ad_r, ag_s, ag_r, al_s, al_r,
):
    n = e_hbm.shape[0]
    k = CLUSTER_COUNT
    Q = C // 2
    full = (R - 1) // 2
    has_half = R % 2 == 0
    half = 1 + full
    r = lax.axis_index("row")
    c = lax.axis_index("col")
    q, b = c // 2, c % 2
    order = plane_order(R)
    place = [order.index(i) for i in range(R)]
    guest_of = {f: look_up(r, [order[(place[i] + f) % R] for i in range(R)]) for f in range(1, half + 1)}
    host_of = {f: look_up(r, [order[(place[i] - f) % R] for i in range(R)]) for f in range(1, half + 1)}
    host_flag = look_up(r, [int(place[i] < R // 2) for i in range(R)])
    is_host = host_flag == 1
    is_guest = host_flag == 0
    fulls = list(range(1, full + 1))
    guests = fulls + ([half] if has_half else [])
    groups = [0] + guests
    last = Q - 1
    near = list(range(1, last))
    far = list(range(1, Q))
    offsets = sorted(range(Q), key=lambda s: (s > 0, -bin(s).count("1")))
    started = []

    def remote(src, dst, ssem, rsem, row, col):
        return pltpu.make_async_remote_copy(
            src_ref=src, dst_ref=dst, send_sem=ssem, recv_sem=rsem,
            device_id=(row, col), device_id_type=MESH,
        )

    def start(copies):
        for copy in copies:
            copy.start()
            started.append(copy)
        return copies

    def hear(copies):
        for copy in copies:
            copy.wait_recv()

    row_peers = [flip(r, t, R) for t in range(R)]
    col_peers = [flip(c, u, C) for u in range(C)]

    partner = col_peers[1]

    def chip_peer(s):
        return col_peers[2 * offsets[s]]

    def slot(s, count=1):
        return pl.ds(s * n, count * n)

    barrier = pltpu.get_barrier_semaphore()
    for f in fulls:
        pl.semaphore_signal(barrier, inc=1, device_id=(guest_of[f], c), device_id_type=MESH)
    if has_half:
        @pl.when(is_host)
        def _():
            pl.semaphore_signal(barrier, inc=1, device_id=(guest_of[half], c), device_id_type=MESH)

    for s in far:
        pl.semaphore_signal(barrier, inc=1, device_id=(r, chip_peer(s)), device_id_type=MESH)
    pl.semaphore_signal(barrier, inc=1, device_id=(r, partner), device_id_type=MESH)
    own = [
        pltpu.make_async_copy(e_hbm, e_row.at[slot(0)], in_sem.at[0]),
        pltpu.make_async_copy(s_hbm, s_row.at[0], in_sem.at[1]),
        pltpu.make_async_copy(e_hbm, e_grp.at[0, 0], in_sem.at[2]),
        pltpu.make_async_copy(s_hbm, s_grp.at[0, 0], in_sem.at[3]),
    ]
    for copy in own:
        copy.start()
    if has_half:
        @pl.when(is_guest)
        def _():
            for core in range(2):
                e_grp[core, half] = jnp.zeros(e_grp.shape[2:], F32)
                s_grp[core, half] = jnp.zeros(s_grp.shape[2:], I32)
                a_grp[core, half] = jnp.zeros(a_grp.shape[2:], F32)

        hz[...] = jnp.zeros_like(hz)
    pl.semaphore_wait(barrier, Q + full + (1 - host_flag if has_half else 0))

    class Spread:
        def __init__(self, srcs, rows, grps, d_s, d_r, g_s, g_r, l_s, l_r, chips):
            self.grps, self.l_s, self.l_r = grps, l_s, l_r
            self.guest = {
                t: [
                    remote(src, grp.at[0, t], ss.at[t - 1], rs.at[t - 1], host_of[t], c)
                    for src, grp, ss, rs in zip(srcs, grps, g_s, g_r)
                ]
                for t in guests
            }
            self.direct = {
                s: [
                    remote(
                        src, row(s) if s else grp.at[1, 0], ss.at[s], rs.at[s],
                        r, chip_peer(s) if s else partner,
                    )
                    for src, row, grp, ss, rs in zip(srcs, rows, grps, d_s, d_r)
                ]
                for s in range(Q)
            }
            for f in fulls:
                start(self.guest[f])
            start(self.direct[0])
            if has_half:
                @pl.when(is_guest)
                def _():
                    for copy in self.guest[half]:
                        copy.start()

            for s in chips:
                start(self.direct[s])

        def relay(self, t):
            return [
                remote(grp.at[0, t], grp.at[1, t], ss.at[t - 1], rs.at[t - 1], r, partner)
                for grp, ss, rs in zip(self.grps, self.l_s, self.l_r)
            ]

        def pass_on(self, t):
            hear(self.guest[t])
            for copy in self.relay(t):
                copy.start()

        def pass_half(self):
            if has_half:
                @pl.when(is_host)
                def _():
                    self.pass_on(half)

        def hear_half(self):
            if has_half:
                @pl.when(is_host)
                def _():
                    hear(self.relay(half))

        def finish(self):
            for f in fulls:
                for copy in self.relay(f):
                    copy.wait_send()
            if has_half:
                @pl.when(is_guest)
                def _():
                    for copy in self.guest[half]:
                        copy.wait_send()

                @pl.when(is_host)
                def _():
                    for copy in self.relay(half):
                        copy.wait_send()

    points = Spread(
        (s_hbm, e_hbm), (lambda s: s_row.at[s], lambda s: e_row.at[slot(s)]), (s_grp, e_grp),
        (sd_s, ed_s), (sd_r, ed_r), (sg_s, eg_s), (sg_r, eg_r), (sl_s, el_s), (sl_r, el_r), range(1, Q),
    )

    B = len(groups)

    def span(core, t0, t1, width=1):
        return slot((core * B + t0) * width, (t1 - t0) * width)

    def put_group(w, core, t, member):
        if has_half and t == half:
            member = jnp.where(is_host, member, 0.0)
        p1, p2 = split2(member)
        for low in range(2):
            at = slot((core * B + t) * 2 + low)
            mb[at, :k] = p1
            if w:
                mb[at, k:] = jnp.zeros_like(p2) if low else p2
        return member

    def put_rows(w, s, member):
        p1, p2 = split2(member)
        ma32[slot(s), :] = member
        ma[slot(s), :k] = p1
        if w:
            ma[slot(s), k:] = p2

    def ready_group(core, t):
        x = e_grp[core, t]
        p1, p2 = split2(-2.0 * x)
        at = span(core, t, t + 1)
        xh[at, :] = p1
        xl[at, :] = p2
        q1, q2 = split2(x * x)
        ones = jnp.ones((8, x.shape[1]), BF16)
        csq[:, at] = nt(ones, q2) + nt(ones, q1) + 1.0
        put_group(0, core, t, seeds_to_member(s_grp[core, t]))

    def ready_rows(s):
        x = e_row[slot(s), :]
        p1, p2 = split2(x)
        eh[s, :n, :] = p1
        eh[s, n:, :] = p2
        rsq[s] = jnp.sum(x * x, axis=1, keepdims=True)

    def ready_seeds(s):
        put_rows(0, s, seeds_to_member(s_row[s]))

    def tile(core, t0, t1, s):
        at = span(core, t0, t1)
        both = nt(eh[s], xh[at, :])
        inner = both[:n] + (both[n:] + nt(eh[s, :n, :], xl[at, :]))
        p1, p2 = split2(jnp.sqrt(rsq[s] + csq[0:1, at] + inner))
        for t in range(t0, t1):
            part = slice((t - t0) * n, (t - t0 + 1) * n)
            dhl[slot(s), slot((core * B + t) * 2)] = p1[:, part]
            dhl[slot(s), slot((core * B + t) * 2 + 1)] = p2[:, part]

    def rows_of(w, core, t0, t1, s0, s1):
        at = span(core, t0, t1, 2)
        d = dhl[slot(s0, s1 - s0), at]
        if w == 0:
            return nn(d, mb[at, :k])
        both = nn(d, mb[at, :])
        return both[:, :k] + both[:, k:]

    def groups_of(w, core, s0, s1):
        rows = slot(s0, s1 - s0)
        both = tn(dhl[rows, span(core, 1, B, 2)], ma[rows, :k] if w == 0 else ma[rows, :])
        if w:
            both = both[:, :k] + both[:, k:]
        return [both[2 * i * n : (2 * i + 1) * n] + both[(2 * i + 1) * n : (2 * i + 2) * n] for i in range(B - 1)]

    def over(member, sums):
        return jnp.sum(member * sums, axis=0, keepdims=True)

    class Sweep:
        def __init__(self, w):
            self.w, self.scatter, self.shares, self.parts = w, {}, {}, []
            count = PIECES if w == 0 else 1
            self.pieces = [pl.ds(h * (n // count), n // count) for h in range(count)]

        def rows(self, s, own_part, guest_part):
            psum[self.w, s] = own_part + guest_part

        def send_rows(self, s):
            w = self.w
            self.scatter[s] = start([
                remote(
                    psum.at[w, s, at], rin.at[w, s, at], rs_s.at[w, h, s], rs_r.at[w, h, s], r, chip_peer(s)
                )
                for h, at in enumerate(self.pieces)
            ])

        def cross(self, t):
            w = self.w
            return remote(cc.at[w, t - 1], ci.at[w, t - 1], cx_s.at[w, t - 1], cx_r.at[w, t - 1], r, partner)

        def away(self, t, h):
            w, at = self.w, self.pieces[h]
            return remote(
                cs.at[w, t - 1, at], cr.at[w, t - 1, at], cz_s.at[w, h, t - 1], cz_r.at[w, h, t - 1], guest_of[t], c
            )

        def cross_groups(self, parts):
            for t in guests:
                cc[self.w, t - 1] = parts[t - 1]
            for t in guests:
                start([self.cross(t)])

        def send_groups(self, parts):
            w = self.w
            for t in guests:
                self.cross(t).wait_recv()
                cs[w, t - 1] = parts[t - 1] + ci[w, t - 1]
                if t == guests[0]:
                    self.send_away(t, 0)
            for h in range(len(self.pieces)):
                for t in guests:
                    if h or t != guests[0]:
                        self.send_away(t, h)

        def send_away(self, t, h):
            if t in fulls:
                start([self.away(t, h)])
            else:
                @pl.when(is_host)
                def _():
                    self.away(t, h).start()

        def total(self):
            w = self.w
            cohesion = self.parts[0]
            for part in self.parts[1:]:
                cohesion = cohesion + part
            az_own[w, 0:1, :] = jnp.sum(ma32[slot(0), :], axis=0, keepdims=True)
            az_own[w, 1:2, :] = cohesion

        def share(self, us):
            w = self.w
            for t in range(R - 1, -1, -1):
                for u in us:
                    if t or u:
                        i = t * C + u
                        self.shares[i] = start([
                            remote(
                                az_own.at[w], az_in.at[w, i], az_s.at[w, i], az_r.at[w, i],
                                row_peers[t], col_peers[u],
                            )
                        ])

        def attraction(self, h):
            w, at = self.w, self.pieces[h]
            total = psum[w, 0, at]
            for s in far:
                hear(self.scatter[s][h : h + 1])
                total = total + rin[w, s, at]
            for f in fulls:
                self.away(f, h).wait_recv()
                total = total + cr[w, f - 1, at]
            if has_half:
                @pl.when(is_guest)
                def _():
                    self.away(half, h).wait_recv()
                    hz[at] = cr[w, half - 1, at]
                total = total + hz[at]
            return total

        def scales(self):
            w = self.w
            for i in self.shares:
                hear(self.shares[i])
            az_in[w, 0] = az_own[w]
            both = jnp.sum(az_in[w], axis=0)
            inverse = 1.0 / both[0:1, :]
            return inverse, (both[1:2, :] * inverse) * (0.5 * inverse)

        def finish(self):
            if has_half:
                @pl.when(is_host)
                def _():
                    for h in range(len(self.pieces)):
                        self.away(half, h).wait_send()

    def logits_of(attraction, scales):
        inverse, shift = scales
        logits = (attraction * inverse - shift) * (-1.0 / ANNEAL_TEMP_VALUE)
        return logits - jnp.max(logits, axis=1, keepdims=True)

    def member_of(attraction, scales):
        top = jnp.exp(logits_of(attraction, scales))
        return top * (1.0 / jnp.sum(top, axis=1, keepdims=True))

    sweep = Sweep(0)
    for copy in own:
        copy.wait()
    ready_seeds(0)
    ready_rows(0)
    ready_group(0, 0)
    tile(0, 0, 1, 0)
    hear(points.direct[0])
    ready_group(1, 0)
    tile(1, 0, 1, 0)
    def next_rows(s, ts):
        hear(points.direct[s])
        ready_seeds(s)
        ready_rows(s)
        for core in range(2):
            for t in ts:
                tile(core, t, t + 1, s)

    for s in near[:1]:
        next_rows(s, [0])
    for f in fulls:
        points.pass_on(f)
        ready_group(0, f)
        for s in [0] + near[:1]:
            tile(0, f, f + 1, s)
    for f in fulls:
        hear(points.relay(f))
        ready_group(1, f)
        for s in [0] + near[:1]:
            tile(1, f, f + 1, s)
    points.pass_half()
    if has_half:
        ready_group(0, half)
        for s in [0] + near[:1]:
            tile(0, half, half + 1, s)
    for s in near[1:]:
        next_rows(s, [0] + fulls)
        if has_half:
            tile(0, half, half + 1, s)
    points.hear_half()
    if has_half:
        ready_group(1, half)
        for s in range(last):
            tile(1, half, half + 1, s)
    both = rows_of(0, 0, 1, B, 0, last) + rows_of(0, 1, 1, B, 0, last)
    mine = rows_of(0, 0, 0, 1, 0, last) + rows_of(0, 1, 0, 1, 0, last)
    for s in range(last):
        own_part, guest_part = mine[s * n : (s + 1) * n], both[s * n : (s + 1) * n]
        sweep.rows(s, own_part, guest_part)
        sweep.parts.append(over(ma32[slot(s), :], own_part + 2.0 * guest_part))
    for s in near:
        sweep.send_rows(s)
    hear(points.direct[last][:1])
    ready_seeds(last)
    hear(points.direct[last][1:])
    ready_rows(last)
    tile(1, 1, B, last)
    sweep.cross_groups(groups_of(0, 1, 0, Q))
    tile(0, 1, B, last)
    parts = groups_of(0, 0, 0, Q)
    for core in range(2):
        tile(core, 0, 1, last)
    own_part = rows_of(0, 0, 0, 1, last, Q) + rows_of(0, 1, 0, 1, last, Q)
    guest_part = rows_of(0, 0, 1, B, last, Q) + rows_of(0, 1, 1, B, last, Q)
    sweep.rows(last, own_part, guest_part)
    sweep.parts.append(over(ma32[slot(last), :], own_part + 2.0 * guest_part))
    sweep.send_groups(parts)
    sweep.send_rows(last)
    sweep.total()
    sweep.share(range(C - 1, -1, -1))

    sums = []
    for h, at in enumerate(sweep.pieces):
        a_own[at] = sweep.attraction(h)
        sums.append(Spread(
            (a_own.at[at],),
            (lambda s, h=h: a_row.at[pl.ds(s * n + h * (n // PIECES), n // PIECES)],),
            (a_grp.at[:, :, at],),
            (ad_s.at[h],), (ad_r.at[h],), (ag_s.at[h],), (ag_r.at[h],), (al_s.at[h],), (al_r.at[h],), far,
        ))
    attraction = a_own[...]
    scales = sweep.scales()
    first, sweep = sweep, Sweep(1)
    own_member = member_of(attraction, scales)
    put_rows(1, 0, own_member)
    put_group(1, 0, 0, own_member)
    for part in sums:
        hear(part.direct[0])
    put_group(1, 1, 0, member_of(a_grp[1, 0], scales))
    r0[...] = rows_of(1, 0, 0, 1, 0, Q) + rows_of(1, 1, 0, 1, 0, Q)
    sweep.parts.append(over(own_member, r0[slot(0), :]))
    for part in sums:
        for f in fulls:
            part.pass_on(f)
    for s in far:
        for part in sums:
            hear(part.direct[s])
        member = member_of(a_row[slot(s), :], scales)
        put_rows(1, s, member)
        sweep.parts.append(over(member, r0[slot(s), :]))
    for part in sums:
        part.pass_half()
    cross = groups_of(1, 1, 0, Q)
    sweep.cross_groups(cross)
    parts = groups_of(1, 0, 0, Q)
    for t in guests:
        sweep.parts.append(over(put_group(1, 0, t, member_of(a_grp[0, t], scales)), 2.0 * parts[t - 1]))
    r1[...] = rows_of(1, 0, 1, B, 0, Q)
    for part in sums:
        for f in fulls:
            hear(part.relay(f))
        part.hear_half()
    for t in guests:
        sweep.parts.append(over(put_group(1, 1, t, member_of(a_grp[1, t], scales)), 2.0 * cross[t - 1]))
    sweep.total()
    sweep.share(range(C - 1, -1, -1))
    sweep.send_groups(parts)
    both = r1[...] + rows_of(1, 1, 1, B, 0, Q)
    for s in far + [0]:
        sweep.rows(s, r0[slot(s), :], both[s * n : (s + 1) * n])
        if s:
            sweep.send_rows(s)
    attraction = sweep.attraction(0)
    logits = logits_of(attraction, sweep.scales())
    o_ref[...] = logits - jnp.log(jnp.sum(jnp.exp(logits), axis=1, keepdims=True))

    for copy in started:
        copy.wait_send()
    for part in [points, first, sweep] + sums:
        part.finish()


def shards(R, C, embedding, seed_cluster):
    n, features = embedding.shape
    k = CLUSTER_COUNT
    Q = C // 2
    B = 1 + (R - 1) // 2 + (R % 2 == 0)
    G = max(B - 1, 1)
    dma = pltpu.SemaphoreType.DMA
    V = pltpu.VMEM
    W = SWEEPS
    return pl.pallas_call(
        functools.partial(kernel, R, C),
        out_shape=jax.ShapeDtypeStruct((n, k), F32),
        in_specs=[pl.BlockSpec(memory_space=pl.ANY)] * 2,
        out_specs=pl.BlockSpec(memory_space=pltpu.VMEM),
        scratch_shapes=[
            V((Q * n, features), F32), V((Q, 1, n), I32), V((2, B, n, features), F32), V((2, B, 1, n), I32),
            V((Q, 2 * n, features), BF16), V((Q, n, 1), F32),
            V((2 * B * n, features), BF16), V((2 * B * n, features), BF16), V((8, 2 * B * n), F32),
            V((Q * n, B * 4 * n), BF16), V((Q * n, 2 * k), BF16), V((Q * n, k), F32), V((B * 4 * n, 2 * k), BF16),
            V((Q * n, k), F32), V((Q * n, k), F32),
            V((W, Q, n, k), F32), V((W, Q, n, k), F32), V((W, G, n, k), F32),
            V((W, G, n, k), F32), V((W, G, n, k), F32), V((W, G, n, k), F32), V((n, k), F32),
            V((n, k), F32), V((Q * n, k), F32), V((2, B, n, k), F32),
            V((W, 2, k), F32), V((W, R * C, 2, k), F32),
            dma((4,)), dma((Q,)), dma((Q,)), dma((G,)), dma((G,)), dma((G,)), dma((G,)),
            dma((Q,)), dma((Q,)), dma((G,)), dma((G,)), dma((G,)), dma((G,)),
            dma((W, G)), dma((W, G)), dma((W, PIECES, G)), dma((W, PIECES, G)), dma((W, PIECES, Q)), dma((W, PIECES, Q)),
            dma((W, R * C)), dma((W, R * C)),
            dma((PIECES, Q)), dma((PIECES, Q)), dma((PIECES, G)), dma((PIECES, G)), dma((PIECES, G)), dma((PIECES, G)),
        ],
        compiler_params=pltpu.CompilerParams(
            collective_id=0, has_side_effects=True, vmem_limit_bytes=56426496
        ),
    )(embedding, seed_cluster.reshape(1, n))


def solution(mesh):
    return jax.shard_map(
        functools.partial(shards, mesh.shape["row"], mesh.shape["col"]),
        mesh=mesh,
        in_specs=(P(("row", "col"), None), P(("row", "col"))),
        out_specs=P(("row", "col"), None),
        check_vma=False,
    )
```

```python
import functools

import jax
import jax.numpy as jnp
from jax import lax
from jax.experimental import pallas as pl
from jax.experimental.pallas import tpu as pltpu
from jax.sharding import PartitionSpec as P

CLUSTER_COUNT = 128
SWEEPS = 2
PIECES = 1
ANNEAL_TEMP_VALUE = 0.02
MESH = pl.DeviceIdType.MESH
F32, BF16, I32 = jnp.float32, jnp.bfloat16, jnp.int32


def plane_order(R):
    return [2, 0, 3, 1] if R == 4 else list(range(R))


def flip(index, offset, size):
    out, bit = 0, 1
    while bit < size:
        out = out + bit * ((index // bit + offset // bit) % 2)
        bit *= 2
    return out


def look_up(index, values):
    out = jnp.int32(values[0])
    for i, value in enumerate(values):
        if i:
            out = jnp.where(index == i, jnp.int32(value), out)
    return out


def split2(x):
    first = x.astype(BF16)
    return first, (x - first.astype(F32)).astype(BF16)


def nt(a, b):
    return lax.dot_general(a, b, (((1,), (1,)), ((), ())), preferred_element_type=F32)


def tn(a, b):
    return lax.dot_general(a, b, (((0,), (0,)), ((), ())), preferred_element_type=F32)


def nn(a, b):
    return jnp.dot(a, b, preferred_element_type=F32)


def seeds_to_member(seeds):
    points = seeds.shape[1]
    labels = lax.broadcasted_iota(I32, (CLUSTER_COUNT, points), 0)
    chosen = jnp.where(labels == seeds, 0.5, 0.0).astype(F32)
    return chosen.T + 0.5 / CLUSTER_COUNT


def kernel(
    R, C, e_hbm, s_hbm, o_ref,
    e_row, s_row, e_grp, s_grp, eh, rsq, xh, xl, csq, dhl, ma, ma32, mb,
    r0, r1, psum, rin, cc, ci, cs, cr, hz, a_own, a_row, a_grp, az_own, az_in,
    in_sem, ed_s, ed_r, eg_s, eg_r, el_s, el_r, sd_s, sd_r, sg_s, sg_r, sl_s, sl_r,
    cx_s, cx_r, cz_s, cz_r, rs_s, rs_r, az_s, az_r, ad_s, ad_r, ag_s, ag_r, al_s, al_r,
):
    n = e_hbm.shape[0]
    k = CLUSTER_COUNT
    Q = C // 2
    full = (R - 1) // 2
    has_half = R % 2 == 0
    half = 1 + full
    r = lax.axis_index("row")
    c = lax.axis_index("col")
    q, b = c // 2, c % 2
    order = plane_order(R)
    place = [order.index(i) for i in range(R)]
    guest_of = {f: look_up(r, [order[(place[i] + f) % R] for i in range(R)]) for f in range(1, half + 1)}
    host_of = {f: look_up(r, [order[(place[i] - f) % R] for i in range(R)]) for f in range(1, half + 1)}
    host_flag = look_up(r, [int(place[i] < R // 2) for i in range(R)])
    is_host = host_flag == 1
    is_guest = host_flag == 0
    fulls = list(range(1, full + 1))
    guests = fulls + ([half] if has_half else [])
    groups = [0] + guests
    last = Q - 1
    near = list(range(1, last))
    far = list(range(1, Q))
    offsets = sorted(range(Q), key=lambda s: (s > 0, -bin(s).count("1")))
    started = []

    def remote(src, dst, ssem, rsem, row, col):
        return pltpu.make_async_remote_copy(
            src_ref=src, dst_ref=dst, send_sem=ssem, recv_sem=rsem,
            device_id=(row, col), device_id_type=MESH,
        )

    def start(copies):
        for copy in copies:
            copy.start()
            started.append(copy)
        return copies

    def hear(copies):
        for copy in copies:
            copy.wait_recv()

    row_peers = [flip(r, t, R) for t in range(R)]
    col_peers = [flip(c, u, C) for u in range(C)]

    partner = col_peers[1]

    def chip_peer(s):
        return col_peers[2 * offsets[s]]

    def slot(s, count=1):
        return pl.ds(s * n, count * n)

    barrier = pltpu.get_barrier_semaphore()
    for f in fulls:
        pl.semaphore_signal(barrier, inc=1, device_id=(guest_of[f], c), device_id_type=MESH)
    if has_half:
        @pl.when(is_host)
        def _():
            pl.semaphore_signal(barrier, inc=1, device_id=(guest_of[half], c), device_id_type=MESH)

    for s in far:
        pl.semaphore_signal(barrier, inc=1, device_id=(r, chip_peer(s)), device_id_type=MESH)
    pl.semaphore_signal(barrier, inc=1, device_id=(r, partner), device_id_type=MESH)
    own = [
        pltpu.make_async_copy(e_hbm, e_row.at[slot(0)], in_sem.at[0]),
        pltpu.make_async_copy(s_hbm, s_row.at[0], in_sem.at[1]),
        pltpu.make_async_copy(e_hbm, e_grp.at[0, 0], in_sem.at[2]),
        pltpu.make_async_copy(s_hbm, s_grp.at[0, 0], in_sem.at[3]),
    ]
    for copy in own:
        copy.start()
    if has_half:
        @pl.when(is_guest)
        def _():
            for core in range(2):
                e_grp[core, half] = jnp.zeros(e_grp.shape[2:], F32)
                s_grp[core, half] = jnp.zeros(s_grp.shape[2:], I32)
                a_grp[core, half] = jnp.zeros(a_grp.shape[2:], F32)

        hz[...] = jnp.zeros_like(hz)
    pl.semaphore_wait(barrier, Q + full + (1 - host_flag if has_half else 0))

    class Spread:
        def __init__(self, srcs, rows, grps, d_s, d_r, g_s, g_r, l_s, l_r, chips):
            self.grps, self.l_s, self.l_r = grps, l_s, l_r
            self.guest = {
                t: [
                    remote(src, grp.at[0, t], ss.at[t - 1], rs.at[t - 1], host_of[t], c)
                    for src, grp, ss, rs in zip(srcs, grps, g_s, g_r)
                ]
                for t in guests
            }
            self.direct = {
                s: [
                    remote(
                        src, row(s) if s else grp.at[1, 0], ss.at[s], rs.at[s],
                        r, chip_peer(s) if s else partner,
                    )
                    for src, row, grp, ss, rs in zip(srcs, rows, grps, d_s, d_r)
                ]
                for s in range(Q)
            }
            for f in fulls:
                start(self.guest[f])
            start(self.direct[0])
            if has_half:
                @pl.when(is_guest)
                def _():
                    for copy in self.guest[half]:
                        copy.start()

            for s in chips:
                start(self.direct[s])

        def relay(self, t):
            return [
                remote(grp.at[0, t], grp.at[1, t], ss.at[t - 1], rs.at[t - 1], r, partner)
                for grp, ss, rs in zip(self.grps, self.l_s, self.l_r)
            ]

        def pass_on(self, t):
            hear(self.guest[t])
            for copy in self.relay(t):
                copy.start()

        def pass_half(self):
            if has_half:
                @pl.when(is_host)
                def _():
                    self.pass_on(half)

        def hear_half(self):
            if has_half:
                @pl.when(is_host)
                def _():
                    hear(self.relay(half))

        def finish(self):
            for f in fulls:
                for copy in self.relay(f):
                    copy.wait_send()
            if has_half:
                @pl.when(is_guest)
                def _():
                    for copy in self.guest[half]:
                        copy.wait_send()

                @pl.when(is_host)
                def _():
                    for copy in self.relay(half):
                        copy.wait_send()

    points = Spread(
        (s_hbm, e_hbm), (lambda s: s_row.at[s], lambda s: e_row.at[slot(s)]), (s_grp, e_grp),
        (sd_s, ed_s), (sd_r, ed_r), (sg_s, eg_s), (sg_r, eg_r), (sl_s, el_s), (sl_r, el_r), range(1, Q),
    )

    B = len(groups)

    def span(core, t0, t1, width=1):
        return slot((core * B + t0) * width, (t1 - t0) * width)

    def put_group(w, core, t, member):
        if has_half and t == half:
            member = jnp.where(is_host, member, 0.0)
        p1, p2 = split2(member)
        for low in range(2):
            at = slot((core * B + t) * 2 + low)
            mb[at, :k] = p1
            if w:
                mb[at, k:] = jnp.zeros_like(p2) if low else p2
        return member

    def put_rows(w, s, member):
        p1, p2 = split2(member)
        ma32[slot(s), :] = member
        ma[slot(s), :k] = p1
        if w:
            ma[slot(s), k:] = p2

    def ready_group(core, t):
        x = e_grp[core, t]
        p1, p2 = split2(-2.0 * x)
        at = span(core, t, t + 1)
        xh[at, :] = p1
        xl[at, :] = p2
        q1, q2 = split2(x * x)
        ones = jnp.ones((8, x.shape[1]), BF16)
        csq[:, at] = nt(ones, q2) + nt(ones, q1) + 1.0
        put_group(0, core, t, seeds_to_member(s_grp[core, t]))

    def ready_rows(s):
        x = e_row[slot(s), :]
        p1, p2 = split2(x)
        eh[s, :n, :] = p1
        eh[s, n:, :] = p2
        rsq[s] = jnp.sum(x * x, axis=1, keepdims=True)

    def ready_seeds(s):
        put_rows(0, s, seeds_to_member(s_row[s]))

    def tile(core, t0, t1, s):
        at = span(core, t0, t1)
        both = nt(eh[s], xh[at, :])
        inner = both[:n] + (both[n:] + nt(eh[s, :n, :], xl[at, :]))
        p1, p2 = split2(jnp.sqrt(rsq[s] + csq[0:1, at] + inner))
        for t in range(t0, t1):
            part = slice((t - t0) * n, (t - t0 + 1) * n)
            dhl[slot(s), slot((core * B + t) * 2)] = p1[:, part]
            dhl[slot(s), slot((core * B + t) * 2 + 1)] = p2[:, part]

    def rows_of(w, core, t0, t1, s0, s1):
        at = span(core, t0, t1, 2)
        d = dhl[slot(s0, s1 - s0), at]
        if w == 0:
            return nn(d, mb[at, :k])
        both = nn(d, mb[at, :])
        return both[:, :k] + both[:, k:]

    def groups_of(w, core, s0, s1):
        rows = slot(s0, s1 - s0)
        both = tn(dhl[rows, span(core, 1, B, 2)], ma[rows, :k] if w == 0 else ma[rows, :])
        if w:
            both = both[:, :k] + both[:, k:]
        return [both[2 * i * n : (2 * i + 1) * n] + both[(2 * i + 1) * n : (2 * i + 2) * n] for i in range(B - 1)]

    def over(member, sums):
        return jnp.sum(member * sums, axis=0, keepdims=True)

    class Sweep:
        def __init__(self, w):
            self.w, self.scatter, self.shares, self.parts = w, {}, {}, []
            count = PIECES if w == 0 else 1
            self.pieces = [pl.ds(h * (n // count), n // count) for h in range(count)]

        def rows(self, s, own_part, guest_part):
            psum[self.w, s] = own_part + guest_part

        def send_rows(self, s):
            w = self.w
            self.scatter[s] = start([
                remote(
                    psum.at[w, s, at], rin.at[w, s, at], rs_s.at[w, h, s], rs_r.at[w, h, s], r, chip_peer(s)
                )
                for h, at in enumerate(self.pieces)
            ])

        def cross(self, t):
            w = self.w
            return remote(cc.at[w, t - 1], ci.at[w, t - 1], cx_s.at[w, t - 1], cx_r.at[w, t - 1], r, partner)

        def away(self, t, h):
            w, at = self.w, self.pieces[h]
            return remote(
                cs.at[w, t - 1, at], cr.at[w, t - 1, at], cz_s.at[w, h, t - 1], cz_r.at[w, h, t - 1], guest_of[t], c
            )

        def cross_groups(self, parts):
            for t in guests:
                cc[self.w, t - 1] = parts[t - 1]
            for t in guests:
                start([self.cross(t)])

        def send_groups(self, parts):
            w = self.w
            for t in guests:
                self.cross(t).wait_recv()
                cs[w, t - 1] = parts[t - 1] + ci[w, t - 1]
                if t == guests[0]:
                    self.send_away(t, 0)
            for h in range(len(self.pieces)):
                for t in guests:
                    if h or t != guests[0]:
                        self.send_away(t, h)

        def send_away(self, t, h):
            if t in fulls:
                start([self.away(t, h)])
            else:
                @pl.when(is_host)
                def _():
                    self.away(t, h).start()

        def total(self):
            w = self.w
            cohesion = self.parts[0]
            for part in self.parts[1:]:
                cohesion = cohesion + part
            az_own[w, 0:1, :] = jnp.sum(ma32[slot(0), :], axis=0, keepdims=True)
            az_own[w, 1:2, :] = cohesion

        def share(self, us):
            w = self.w
            for t in range(R - 1, -1, -1):
                for u in us:
                    if t or u:
                        i = t * C + u
                        self.shares[i] = start([
                            remote(
                                az_own.at[w], az_in.at[w, i], az_s.at[w, i], az_r.at[w, i],
                                row_peers[t], col_peers[u],
                            )
                        ])

        def attraction(self, h):
            w, at = self.w, self.pieces[h]
            total = psum[w, 0, at]
            for s in far:
                hear(self.scatter[s][h : h + 1])
                total = total + rin[w, s, at]
            for f in fulls:
                self.away(f, h).wait_recv()
                total = total + cr[w, f - 1, at]
            if has_half:
                @pl.when(is_guest)
                def _():
                    self.away(half, h).wait_recv()
                    hz[at] = cr[w, half - 1, at]
                total = total + hz[at]
            return total

        def scales(self):
            w = self.w
            for i in self.shares:
                hear(self.shares[i])
            az_in[w, 0] = az_own[w]
            both = jnp.sum(az_in[w], axis=0)
            inverse = 1.0 / both[0:1, :]
            return inverse, (both[1:2, :] * inverse) * (0.5 * inverse)

        def finish(self):
            if has_half:
                @pl.when(is_host)
                def _():
                    for h in range(len(self.pieces)):
                        self.away(half, h).wait_send()

    def logits_of(attraction, scales):
        inverse, shift = scales
        logits = (attraction * inverse - shift) * (-1.0 / ANNEAL_TEMP_VALUE)
        return logits - jnp.max(logits, axis=1, keepdims=True)

    def member_of(attraction, scales):
        top = jnp.exp(logits_of(attraction, scales))
        return top * (1.0 / jnp.sum(top, axis=1, keepdims=True))

    sweep = Sweep(0)
    for copy in own:
        copy.wait()
    ready_seeds(0)
    ready_rows(0)
    ready_group(0, 0)
    tile(0, 0, 1, 0)
    hear(points.direct[0])
    ready_group(1, 0)
    tile(1, 0, 1, 0)
    def next_rows(s, ts):
        hear(points.direct[s])
        ready_seeds(s)
        ready_rows(s)
        for core in range(2):
            for t in ts:
                tile(core, t, t + 1, s)

    for s in near[:1]:
        next_rows(s, [0])
    for f in fulls:
        points.pass_on(f)
        ready_group(0, f)
        for s in [0] + near[:1]:
            tile(0, f, f + 1, s)
    for f in fulls:
        hear(points.relay(f))
        ready_group(1, f)
        for s in [0] + near[:1]:
            tile(1, f, f + 1, s)
    points.pass_half()
    if has_half:
        ready_group(0, half)
        for s in [0] + near[:1]:
            tile(0, half, half + 1, s)
    for s in near[1:]:
        next_rows(s, [0] + fulls)
        if has_half:
            tile(0, half, half + 1, s)
    points.hear_half()
    if has_half:
        ready_group(1, half)
        for s in range(last):
            tile(1, half, half + 1, s)
    both = rows_of(0, 0, 1, B, 0, last) + rows_of(0, 1, 1, B, 0, last)
    mine = rows_of(0, 0, 0, 1, 0, last) + rows_of(0, 1, 0, 1, 0, last)
    for s in range(last):
        own_part, guest_part = mine[s * n : (s + 1) * n], both[s * n : (s + 1) * n]
        sweep.rows(s, own_part, guest_part)
        sweep.parts.append(over(ma32[slot(s), :], own_part + 2.0 * guest_part))
    for s in near:
        sweep.send_rows(s)
    hear(points.direct[last][:1])
    ready_seeds(last)
    hear(points.direct[last][1:])
    ready_rows(last)
    tile(1, 1, B, last)
    tile(0, 1, B, last)
    sweep.cross_groups(groups_of(0, 1, 0, Q))
    for core in range(2):
        tile(core, 0, 1, last)
    parts = groups_of(0, 0, 0, Q)
    sweep.send_groups(parts)
    own_part = rows_of(0, 0, 0, 1, last, Q) + rows_of(0, 1, 0, 1, last, Q)
    guest_part = rows_of(0, 0, 1, B, last, Q) + rows_of(0, 1, 1, B, last, Q)
    sweep.rows(last, own_part, guest_part)
    sweep.parts.append(over(ma32[slot(last), :], own_part + 2.0 * guest_part))
    sweep.send_rows(last)
    sweep.total()
    sweep.share(range(C - 1, -1, -1))

    sums = []
    for h, at in enumerate(sweep.pieces):
        a_own[at] = sweep.attraction(h)
        sums.append(Spread(
            (a_own.at[at],),
            (lambda s, h=h: a_row.at[pl.ds(s * n + h * (n // PIECES), n // PIECES)],),
            (a_grp.at[:, :, at],),
            (ad_s.at[h],), (ad_r.at[h],), (ag_s.at[h],), (ag_r.at[h],), (al_s.at[h],), (al_r.at[h],), far,
        ))
    attraction = a_own[...]
    scales = sweep.scales()
    first, sweep = sweep, Sweep(1)
    own_member = member_of(attraction, scales)
    put_rows(1, 0, own_member)
    put_group(1, 0, 0, own_member)
    for part in sums:
        hear(part.direct[0])
    put_group(1, 1, 0, member_of(a_grp[1, 0], scales))
    r0[...] = rows_of(1, 0, 0, 1, 0, Q) + rows_of(1, 1, 0, 1, 0, Q)
    sweep.parts.append(over(own_member, r0[slot(0), :]))
    for part in sums:
        for f in fulls:
            part.pass_on(f)
    for s in far:
        for part in sums:
            hear(part.direct[s])
        member = member_of(a_row[slot(s), :], scales)
        put_rows(1, s, member)
        sweep.parts.append(over(member, r0[slot(s), :]))
    for part in sums:
        part.pass_half()
    cross = groups_of(1, 1, 0, Q)
    sweep.cross_groups(cross)
    parts = groups_of(1, 0, 0, Q)
    for t in guests:
        sweep.parts.append(over(put_group(1, 0, t, member_of(a_grp[0, t], scales)), 2.0 * parts[t - 1]))
    r1[...] = rows_of(1, 0, 1, B, 0, Q)
    for part in sums:
        for f in fulls:
            hear(part.relay(f))
        part.hear_half()
    for t in guests:
        sweep.parts.append(over(put_group(1, 1, t, member_of(a_grp[1, t], scales)), 2.0 * cross[t - 1]))
    sweep.total()
    sweep.share(range(C - 1, -1, -1))
    sweep.send_groups(parts)
    both = r1[...] + rows_of(1, 1, 1, B, 0, Q)
    for s in far + [0]:
        sweep.rows(s, r0[slot(s), :], both[s * n : (s + 1) * n])
        if s:
            sweep.send_rows(s)
    attraction = sweep.attraction(0)
    logits = logits_of(attraction, sweep.scales())
    o_ref[...] = logits - jnp.log(jnp.sum(jnp.exp(logits), axis=1, keepdims=True))

    for copy in started:
        copy.wait_send()
    for part in [points, first, sweep] + sums:
        part.finish()


def shards(R, C, embedding, seed_cluster):
    n, features = embedding.shape
    k = CLUSTER_COUNT
    Q = C // 2
    B = 1 + (R - 1) // 2 + (R % 2 == 0)
    G = max(B - 1, 1)
    dma = pltpu.SemaphoreType.DMA
    V = pltpu.VMEM
    W = SWEEPS
    return pl.pallas_call(
        functools.partial(kernel, R, C),
        out_shape=jax.ShapeDtypeStruct((n, k), F32),
        in_specs=[pl.BlockSpec(memory_space=pl.ANY)] * 2,
        out_specs=pl.BlockSpec(memory_space=pltpu.VMEM),
        scratch_shapes=[
            V((Q * n, features), F32), V((Q, 1, n), I32), V((2, B, n, features), F32), V((2, B, 1, n), I32),
            V((Q, 2 * n, features), BF16), V((Q, n, 1), F32),
            V((2 * B * n, features), BF16), V((2 * B * n, features), BF16), V((8, 2 * B * n), F32),
            V((Q * n, B * 4 * n), BF16), V((Q * n, 2 * k), BF16), V((Q * n, k), F32), V((B * 4 * n, 2 * k), BF16),
            V((Q * n, k), F32), V((Q * n, k), F32),
            V((W, Q, n, k), F32), V((W, Q, n, k), F32), V((W, G, n, k), F32),
            V((W, G, n, k), F32), V((W, G, n, k), F32), V((W, G, n, k), F32), V((n, k), F32),
            V((n, k), F32), V((Q * n, k), F32), V((2, B, n, k), F32),
            V((W, 2, k), F32), V((W, R * C, 2, k), F32),
            dma((4,)), dma((Q,)), dma((Q,)), dma((G,)), dma((G,)), dma((G,)), dma((G,)),
            dma((Q,)), dma((Q,)), dma((G,)), dma((G,)), dma((G,)), dma((G,)),
            dma((W, G)), dma((W, G)), dma((W, PIECES, G)), dma((W, PIECES, G)), dma((W, PIECES, Q)), dma((W, PIECES, Q)),
            dma((W, R * C)), dma((W, R * C)),
            dma((PIECES, Q)), dma((PIECES, Q)), dma((PIECES, G)), dma((PIECES, G)), dma((PIECES, G)), dma((PIECES, G)),
        ],
        compiler_params=pltpu.CompilerParams(
            collective_id=0, has_side_effects=True, vmem_limit_bytes=56426496
        ),
    )(embedding, seed_cluster.reshape(1, n))


def solution(mesh):
    return jax.shard_map(
        functools.partial(shards, mesh.shape["row"], mesh.shape["col"]),
        mesh=mesh,
        in_specs=(P(("row", "col"), None), P(("row", "col"))),
        out_specs=P(("row", "col"), None),
        check_vma=False,
    )
```

```python
import functools

import jax
import jax.numpy as jnp
from jax import lax
from jax.experimental import pallas as pl
from jax.experimental.pallas import tpu as pltpu
from jax.sharding import PartitionSpec as P

CLUSTER_COUNT = 128
SWEEPS = 2
PIECES = 1
ANNEAL_TEMP_VALUE = 0.02
MESH = pl.DeviceIdType.MESH
F32, BF16, I32 = jnp.float32, jnp.bfloat16, jnp.int32


def plane_order(R):
    return [2, 0, 3, 1] if R == 4 else list(range(R))


def flip(index, offset, size):
    out, bit = 0, 1
    while bit < size:
        out = out + bit * ((index // bit + offset // bit) % 2)
        bit *= 2
    return out


def look_up(index, values):
    out = jnp.int32(values[0])
    for i, value in enumerate(values):
        if i:
            out = jnp.where(index == i, jnp.int32(value), out)
    return out


def split2(x):
    first = x.astype(BF16)
    return first, (x - first.astype(F32)).astype(BF16)


def nt(a, b):
    return lax.dot_general(a, b, (((1,), (1,)), ((), ())), preferred_element_type=F32)


def tn(a, b):
    return lax.dot_general(a, b, (((0,), (0,)), ((), ())), preferred_element_type=F32)


def nn(a, b):
    return jnp.dot(a, b, preferred_element_type=F32)


def seeds_to_member(seeds):
    points = seeds.shape[1]
    labels = lax.broadcasted_iota(I32, (CLUSTER_COUNT, points), 0)
    chosen = jnp.where(labels == seeds, 0.5, 0.0).astype(F32)
    return chosen.T + 0.5 / CLUSTER_COUNT


def kernel(
    R, C, e_hbm, s_hbm, o_ref,
    e_row, s_row, e_grp, s_grp, eh, rsq, xh, xl, csq, dhl, ma, ma32, mb,
    r0, r1, psum, rin, cc, ci, cs, cr, hz, a_own, a_row, a_grp, az_own, az_in,
    in_sem, ed_s, ed_r, eg_s, eg_r, el_s, el_r, sd_s, sd_r, sg_s, sg_r, sl_s, sl_r,
    cx_s, cx_r, cz_s, cz_r, rs_s, rs_r, az_s, az_r, ad_s, ad_r, ag_s, ag_r, al_s, al_r,
):
    n = e_hbm.shape[0]
    k = CLUSTER_COUNT
    Q = C // 2
    full = (R - 1) // 2
    has_half = R % 2 == 0
    half = 1 + full
    r = lax.axis_index("row")
    c = lax.axis_index("col")
    q, b = c // 2, c % 2
    order = plane_order(R)
    place = [order.index(i) for i in range(R)]
    guest_of = {f: look_up(r, [order[(place[i] + f) % R] for i in range(R)]) for f in range(1, half + 1)}
    host_of = {f: look_up(r, [order[(place[i] - f) % R] for i in range(R)]) for f in range(1, half + 1)}
    host_flag = look_up(r, [int(place[i] < R // 2) for i in range(R)])
    is_host = host_flag == 1
    is_guest = host_flag == 0
    fulls = list(range(1, full + 1))
    guests = fulls + ([half] if has_half else [])
    groups = [0] + guests
    last = Q - 1
    near = list(range(1, last))
    far = list(range(1, Q))
    offsets = sorted(range(Q), key=lambda s: (s > 0, -bin(s).count("1")))
    started = []

    def remote(src, dst, ssem, rsem, row, col):
        return pltpu.make_async_remote_copy(
            src_ref=src, dst_ref=dst, send_sem=ssem, recv_sem=rsem,
            device_id=(row, col), device_id_type=MESH,
        )

    def start(copies):
        for copy in copies:
            copy.start()
            started.append(copy)
        return copies

    def hear(copies):
        for copy in copies:
            copy.wait_recv()

    row_peers = [flip(r, t, R) for t in range(R)]
    col_peers = [flip(c, u, C) for u in range(C)]

    partner = col_peers[1]

    def chip_peer(s):
        return col_peers[2 * offsets[s]]

    def slot(s, count=1):
        return pl.ds(s * n, count * n)

    barrier = pltpu.get_barrier_semaphore()
    for f in fulls:
        pl.semaphore_signal(barrier, inc=1, device_id=(guest_of[f], c), device_id_type=MESH)
    if has_half:
        @pl.when(is_host)
        def _():
            pl.semaphore_signal(barrier, inc=1, device_id=(guest_of[half], c), device_id_type=MESH)

    for s in far:
        pl.semaphore_signal(barrier, inc=1, device_id=(r, chip_peer(s)), device_id_type=MESH)
    pl.semaphore_signal(barrier, inc=1, device_id=(r, partner), device_id_type=MESH)
    own = [
        pltpu.make_async_copy(e_hbm, e_row.at[slot(0)], in_sem.at[0]),
        pltpu.make_async_copy(s_hbm, s_row.at[0], in_sem.at[1]),
        pltpu.make_async_copy(e_hbm, e_grp.at[0, 0], in_sem.at[2]),
        pltpu.make_async_copy(s_hbm, s_grp.at[0, 0], in_sem.at[3]),
    ]
    for copy in own:
        copy.start()
    if has_half:
        @pl.when(is_guest)
        def _():
            for core in range(2):
                e_grp[core, half] = jnp.zeros(e_grp.shape[2:], F32)
                s_grp[core, half] = jnp.zeros(s_grp.shape[2:], I32)
                a_grp[core, half] = jnp.zeros(a_grp.shape[2:], F32)

        hz[...] = jnp.zeros_like(hz)
    pl.semaphore_wait(barrier, Q + full + (1 - host_flag if has_half else 0))

    class Spread:
        def __init__(self, srcs, rows, grps, d_s, d_r, g_s, g_r, l_s, l_r, chips):
            self.grps, self.l_s, self.l_r = grps, l_s, l_r
            self.guest = {
                t: [
                    remote(src, grp.at[0, t], ss.at[t - 1], rs.at[t - 1], host_of[t], c)
                    for src, grp, ss, rs in zip(srcs, grps, g_s, g_r)
                ]
                for t in guests
            }
            self.direct = {
                s: [
                    remote(
                        src, row(s) if s else grp.at[1, 0], ss.at[s], rs.at[s],
                        r, chip_peer(s) if s else partner,
                    )
                    for src, row, grp, ss, rs in zip(srcs, rows, grps, d_s, d_r)
                ]
                for s in range(Q)
            }
            for f in fulls:
                start(self.guest[f])
            start(self.direct[0])
            if has_half:
                @pl.when(is_guest)
                def _():
                    for copy in self.guest[half]:
                        copy.start()

            for s in chips:
                start(self.direct[s])

        def relay(self, t):
            return [
                remote(grp.at[0, t], grp.at[1, t], ss.at[t - 1], rs.at[t - 1], r, partner)
                for grp, ss, rs in zip(self.grps, self.l_s, self.l_r)
            ]

        def pass_on(self, t):
            hear(self.guest[t])
            for copy in self.relay(t):
                copy.start()

        def pass_half(self):
            if has_half:
                @pl.when(is_host)
                def _():
                    self.pass_on(half)

        def hear_half(self):
            if has_half:
                @pl.when(is_host)
                def _():
                    hear(self.relay(half))

        def finish(self):
            for f in fulls:
                for copy in self.relay(f):
                    copy.wait_send()
            if has_half:
                @pl.when(is_guest)
                def _():
                    for copy in self.guest[half]:
                        copy.wait_send()

                @pl.when(is_host)
                def _():
                    for copy in self.relay(half):
                        copy.wait_send()

    points = Spread(
        (s_hbm, e_hbm), (lambda s: s_row.at[s], lambda s: e_row.at[slot(s)]), (s_grp, e_grp),
        (sd_s, ed_s), (sd_r, ed_r), (sg_s, eg_s), (sg_r, eg_r), (sl_s, el_s), (sl_r, el_r), range(1, Q),
    )

    B = len(groups)

    def span(core, t0, t1, width=1):
        return slot((core * B + t0) * width, (t1 - t0) * width)

    def put_group(w, core, t, member):
        if has_half and t == half:
            member = jnp.where(is_host, member, 0.0)
        p1, p2 = split2(member)
        for low in range(2):
            at = slot((core * B + t) * 2 + low)
            mb[at, :k] = p1
            if w:
                mb[at, k:] = jnp.zeros_like(p2) if low else p2
        return member

    def put_rows(w, s, member):
        p1, p2 = split2(member)
        ma32[slot(s), :] = member
        ma[slot(s), :k] = p1
        if w:
            ma[slot(s), k:] = p2

    def ready_group(core, t):
        x = e_grp[core, t]
        p1, p2 = split2(-2.0 * x)
        at = span(core, t, t + 1)
        xh[at, :] = p1
        xl[at, :] = p2
        q1, q2 = split2(x * x)
        ones = jnp.ones((8, x.shape[1]), BF16)
        csq[:, at] = nt(ones, q2) + nt(ones, q1) + 1.0
        put_group(0, core, t, seeds_to_member(s_grp[core, t]))

    def ready_rows(s):
        x = e_row[slot(s), :]
        p1, p2 = split2(x)
        eh[s, :n, :] = p1
        eh[s, n:, :] = p2
        rsq[s] = jnp.sum(x * x, axis=1, keepdims=True)

    def ready_seeds(s):
        put_rows(0, s, seeds_to_member(s_row[s]))

    def tile(core, t0, t1, s):
        at = span(core, t0, t1)
        both = nt(eh[s], xh[at, :])
        inner = both[:n] + (both[n:] + nt(eh[s, :n, :], xl[at, :]))
        p1, p2 = split2(jnp.sqrt(rsq[s] + csq[0:1, at] + inner))
        for t in range(t0, t1):
            part = slice((t - t0) * n, (t - t0 + 1) * n)
            dhl[slot(s), slot((core * B + t) * 2)] = p1[:, part]
            dhl[slot(s), slot((core * B + t) * 2 + 1)] = p2[:, part]

    def rows_of(w, core, t0, t1, s0, s1):
        at = span(core, t0, t1, 2)
        d = dhl[slot(s0, s1 - s0), at]
        if w == 0:
            return nn(d, mb[at, :k])
        both = nn(d, mb[at, :])
        return both[:, :k] + both[:, k:]

    def groups_of(w, core, s0, s1):
        rows = slot(s0, s1 - s0)
        both = tn(dhl[rows, span(core, 1, B, 2)], ma[rows, :k] if w == 0 else ma[rows, :])
        if w:
            both = both[:, :k] + both[:, k:]
        return [both[2 * i * n : (2 * i + 1) * n] + both[(2 * i + 1) * n : (2 * i + 2) * n] for i in range(B - 1)]

    def over(member, sums):
        return jnp.sum(member * sums, axis=0, keepdims=True)

    class Sweep:
        def __init__(self, w):
            self.w, self.scatter, self.shares, self.parts = w, {}, {}, []
            count = PIECES if w == 0 else 1
            self.pieces = [pl.ds(h * (n // count), n // count) for h in range(count)]

        def rows(self, s, own_part, guest_part):
            psum[self.w, s] = own_part + guest_part

        def send_rows(self, s):
            w = self.w
            self.scatter[s] = start([
                remote(
                    psum.at[w, s, at], rin.at[w, s, at], rs_s.at[w, h, s], rs_r.at[w, h, s], r, chip_peer(s)
                )
                for h, at in enumerate(self.pieces)
            ])

        def cross(self, t):
            w = self.w
            return remote(cc.at[w, t - 1], ci.at[w, t - 1], cx_s.at[w, t - 1], cx_r.at[w, t - 1], r, partner)

        def away(self, t, h):
            w, at = self.w, self.pieces[h]
            return remote(
                cs.at[w, t - 1, at], cr.at[w, t - 1, at], cz_s.at[w, h, t - 1], cz_r.at[w, h, t - 1], guest_of[t], c
            )

        def cross_groups(self, parts):
            for t in guests:
                cc[self.w, t - 1] = parts[t - 1]
            for t in guests:
                start([self.cross(t)])

        def send_groups(self, parts):
            w = self.w
            for t in guests:
                self.cross(t).wait_recv()
                cs[w, t - 1] = parts[t - 1] + ci[w, t - 1]
                if t == guests[0]:
                    self.send_away(t, 0)
            for h in range(len(self.pieces)):
                for t in guests:
                    if h or t != guests[0]:
                        self.send_away(t, h)

        def send_away(self, t, h):
            if t in fulls:
                start([self.away(t, h)])
            else:
                @pl.when(is_host)
                def _():
                    self.away(t, h).start()

        def total(self):
            w = self.w
            cohesion = self.parts[0]
            for part in self.parts[1:]:
                cohesion = cohesion + part
            az_own[w, 0:1, :] = jnp.sum(ma32[slot(0), :], axis=0, keepdims=True)
            az_own[w, 1:2, :] = cohesion

        def share(self, us):
            w = self.w
            for t in range(R - 1, -1, -1):
                for u in us:
                    if t or u:
                        i = t * C + u
                        self.shares[i] = start([
                            remote(
                                az_own.at[w], az_in.at[w, i], az_s.at[w, i], az_r.at[w, i],
                                row_peers[t], col_peers[u],
                            )
                        ])

        def attraction(self, h):
            w, at = self.w, self.pieces[h]
            total = psum[w, 0, at]
            for s in far:
                hear(self.scatter[s][h : h + 1])
                total = total + rin[w, s, at]
            for f in fulls:
                self.away(f, h).wait_recv()
                total = total + cr[w, f - 1, at]
            if has_half:
                @pl.when(is_guest)
                def _():
                    self.away(half, h).wait_recv()
                    hz[at] = cr[w, half - 1, at]
                total = total + hz[at]
            return total

        def scales(self):
            w = self.w
            for i in self.shares:
                hear(self.shares[i])
            az_in[w, 0] = az_own[w]
            both = jnp.sum(az_in[w], axis=0)
            inverse = 1.0 / both[0:1, :]
            return inverse, (both[1:2, :] * inverse) * (0.5 * inverse)

        def finish(self):
            if has_half:
                @pl.when(is_host)
                def _():
                    for h in range(len(self.pieces)):
                        self.away(half, h).wait_send()

    def logits_of(attraction, scales):
        inverse, shift = scales
        logits = (attraction * inverse - shift) * (-1.0 / ANNEAL_TEMP_VALUE)
        return logits - jnp.max(logits, axis=1, keepdims=True)

    def member_of(attraction, scales):
        top = jnp.exp(logits_of(attraction, scales))
        return top * (1.0 / jnp.sum(top, axis=1, keepdims=True))

    sweep = Sweep(0)
    for copy in own:
        copy.wait()
    ready_seeds(0)
    ready_rows(0)
    ready_group(0, 0)
    tile(0, 0, 1, 0)
    hear(points.direct[0])
    ready_group(1, 0)
    tile(1, 0, 1, 0)
    def next_rows(s, ts):
        hear(points.direct[s])
        ready_seeds(s)
        ready_rows(s)
        for core in range(2):
            for t in ts:
                tile(core, t, t + 1, s)

    for s in near[:1]:
        next_rows(s, [0])
    for f in fulls:
        points.pass_on(f)
        ready_group(0, f)
        for s in [0] + near[:1]:
            tile(0, f, f + 1, s)
    for f in fulls:
        hear(points.relay(f))
        ready_group(1, f)
        for s in [0] + near[:1]:
            tile(1, f, f + 1, s)
    points.pass_half()
    if has_half:
        ready_group(0, half)
        for s in [0] + near[:1]:
            tile(0, half, half + 1, s)
    for s in near[1:]:
        next_rows(s, [0] + fulls)
        if has_half:
            tile(0, half, half + 1, s)
    points.hear_half()
    if has_half:
        ready_group(1, half)
        for s in range(last):
            tile(1, half, half + 1, s)
    both = rows_of(0, 0, 1, B, 0, last) + rows_of(0, 1, 1, B, 0, last)
    mine = rows_of(0, 0, 0, 1, 0, last) + rows_of(0, 1, 0, 1, 0, last)
    for s in range(last):
        own_part, guest_part = mine[s * n : (s + 1) * n], both[s * n : (s + 1) * n]
        sweep.rows(s, own_part, guest_part)
        sweep.parts.append(over(ma32[slot(s), :], own_part + 2.0 * guest_part))
    for s in near:
        sweep.send_rows(s)
    hear(points.direct[last][:1])
    ready_seeds(last)
    hear(points.direct[last][1:])
    ready_rows(last)
    tile(1, 1, B, last)
    tile(0, 1, B, last)
    sweep.cross_groups(groups_of(0, 1, 0, Q))
    for core in range(2):
        tile(core, 0, 1, last)
    parts = groups_of(0, 0, 0, Q)
    sweep.send_groups(parts)
    own_part = rows_of(0, 0, 0, 1, last, Q) + rows_of(0, 1, 0, 1, last, Q)
    guest_part = rows_of(0, 0, 1, B, last, Q) + rows_of(0, 1, 1, B, last, Q)
    sweep.rows(last, own_part, guest_part)
    sweep.parts.append(over(ma32[slot(last), :], own_part + 2.0 * guest_part))
    sweep.send_rows(last)
    sweep.total()
    sweep.share(range(C - 1, -1, -1))

    sums = []
    for h, at in enumerate(sweep.pieces):
        a_own[at] = sweep.attraction(h)
        sums.append(Spread(
            (a_own.at[at],),
            (lambda s, h=h: a_row.at[pl.ds(s * n + h * (n // PIECES), n // PIECES)],),
            (a_grp.at[:, :, at],),
            (ad_s.at[h],), (ad_r.at[h],), (ag_s.at[h],), (ag_r.at[h],), (al_s.at[h],), (al_r.at[h],), far,
        ))
    attraction = a_own[...]
    old = len(started)
    scales = sweep.scales()
    first, sweep = sweep, Sweep(1)
    own_member = member_of(attraction, scales)
    put_rows(1, 0, own_member)
    put_group(1, 0, 0, own_member)
    for part in sums:
        hear(part.direct[0])
    put_group(1, 1, 0, member_of(a_grp[1, 0], scales))
    r0[...] = rows_of(1, 0, 0, 1, 0, Q) + rows_of(1, 1, 0, 1, 0, Q)
    sweep.parts.append(over(own_member, r0[slot(0), :]))
    for part in sums:
        for f in fulls:
            part.pass_on(f)
    for s in far:
        for part in sums:
            hear(part.direct[s])
        member = member_of(a_row[slot(s), :], scales)
        put_rows(1, s, member)
        sweep.parts.append(over(member, r0[slot(s), :]))
    for part in sums:
        part.pass_half()
    cross = groups_of(1, 1, 0, Q)
    sweep.cross_groups(cross)
    parts = groups_of(1, 0, 0, Q)
    for t in guests:
        sweep.parts.append(over(put_group(1, 0, t, member_of(a_grp[0, t], scales)), 2.0 * parts[t - 1]))
    r1[...] = rows_of(1, 0, 1, B, 0, Q)
    for part in sums:
        for f in fulls:
            hear(part.relay(f))
        part.hear_half()
    for t in guests:
        sweep.parts.append(over(put_group(1, 1, t, member_of(a_grp[1, t], scales)), 2.0 * cross[t - 1]))
    sweep.total()
    sweep.share(range(C - 1, -1, -1))
    sweep.send_groups(parts)
    both = r1[...] + rows_of(1, 1, 1, B, 0, Q)
    for s in far + [0]:
        sweep.rows(s, r0[slot(s), :], both[s * n : (s + 1) * n])
        if s:
            sweep.send_rows(s)
    for copy in started[:old]:
        copy.wait_send()
    attraction = sweep.attraction(0)
    logits = logits_of(attraction, sweep.scales())
    o_ref[...] = logits - jnp.log(jnp.sum(jnp.exp(logits), axis=1, keepdims=True))

    for copy in started[old:]:
        copy.wait_send()
    for part in [points, first, sweep] + sums:
        part.finish()


def shards(R, C, embedding, seed_cluster):
    n, features = embedding.shape
    k = CLUSTER_COUNT
    Q = C // 2
    B = 1 + (R - 1) // 2 + (R % 2 == 0)
    G = max(B - 1, 1)
    dma = pltpu.SemaphoreType.DMA
    V = pltpu.VMEM
    W = SWEEPS
    return pl.pallas_call(
        functools.partial(kernel, R, C),
        out_shape=jax.ShapeDtypeStruct((n, k), F32),
        in_specs=[pl.BlockSpec(memory_space=pl.ANY)] * 2,
        out_specs=pl.BlockSpec(memory_space=pltpu.VMEM),
        scratch_shapes=[
            V((Q * n, features), F32), V((Q, 1, n), I32), V((2, B, n, features), F32), V((2, B, 1, n), I32),
            V((Q, 2 * n, features), BF16), V((Q, n, 1), F32),
            V((2 * B * n, features), BF16), V((2 * B * n, features), BF16), V((8, 2 * B * n), F32),
            V((Q * n, B * 4 * n), BF16), V((Q * n, 2 * k), BF16), V((Q * n, k), F32), V((B * 4 * n, 2 * k), BF16),
            V((Q * n, k), F32), V((Q * n, k), F32),
            V((W, Q, n, k), F32), V((W, Q, n, k), F32), V((W, G, n, k), F32),
            V((W, G, n, k), F32), V((W, G, n, k), F32), V((W, G, n, k), F32), V((n, k), F32),
            V((n, k), F32), V((Q * n, k), F32), V((2, B, n, k), F32),
            V((W, 2, k), F32), V((W, R * C, 2, k), F32),
            dma((4,)), dma((Q,)), dma((Q,)), dma((G,)), dma((G,)), dma((G,)), dma((G,)),
            dma((Q,)), dma((Q,)), dma((G,)), dma((G,)), dma((G,)), dma((G,)),
            dma((W, G)), dma((W, G)), dma((W, PIECES, G)), dma((W, PIECES, G)), dma((W, PIECES, Q)), dma((W, PIECES, Q)),
            dma((W, R * C)), dma((W, R * C)),
            dma((PIECES, Q)), dma((PIECES, Q)), dma((PIECES, G)), dma((PIECES, G)), dma((PIECES, G)), dma((PIECES, G)),
        ],
        compiler_params=pltpu.CompilerParams(
            collective_id=0, has_side_effects=True, vmem_limit_bytes=56426496
        ),
    )(embedding, seed_cluster.reshape(1, n))


def solution(mesh):
    return jax.shard_map(
        functools.partial(shards, mesh.shape["row"], mesh.shape["col"]),
        mesh=mesh,
        in_specs=(P(("row", "col"), None), P(("row", "col"))),
        out_specs=P(("row", "col"), None),
        check_vma=False,
    )
```
